32 devices in a mesh: dp: 4 (over y, x), section: 8 (over z, core).
Axes of the slice: x: 2, y: 2, z: 4, core: 2. Of those that a mesh axis runs over, the one named last changes fastest.
Arguments:
- inputs: bfloat16 [2, 512, 2048], P(None, 'dp'), may hold values from -6 to 6
- cotangent: bfloat16 [2, 512, 2048], P(None, 'dp'), may hold values from -6 to 6
- w_prev: float32 [8, 2048, 2048], P('section', None, 'dp'), may hold values from -6 to 6
- w_now: float32 [8, 2048, 2048], P('section', None, 'dp'), may hold values from -6 to 6
- grads_prev: bfloat16 [4, 8, 2048, 2048], P('dp', 'section'), may hold values from -6 to 6
Outputs:
- w_next: float32 [8, 2048, 2048], P('section', None, 'dp')
- grads_next: bfloat16 [4, 8, 2048, 2048], P('dp', 'section')
The draws below stay inside these ranges and needn't reach their ends.
All inputs are finite; a program needn't handle non-finite values.
Results may differ from the reference program's by a relative error of at most 0.02.
Values may be sent and summed in bfloat16 or wider, within the bound.
A program may use at most 128 MiB of HBM per device.

```python
import jax
import jax.numpy as jnp
from jax import lax

D = 2048
MB = 2
TOKENS = 512
SECTIONS = 8
N_DP = 4


def raised(drawn, stream_key, source, target, parts, factor):
    owner, partner = [(jnp.arange(drawn.shape[axis_at]) // (drawn.shape[axis_at] // parts)).reshape([-1 if axis == axis_at else 1 for axis in range(drawn.ndim)]) for axis_at in (source, target)]
    chosen = jax.random.permutation(stream_key, parts)[partner]
    strong = (owner == chosen) | (owner == (partner + parts // 2) % parts)
    return jnp.where(strong, factor * drawn, drawn)


def levels(stream_key, shape, pieces, least, top_value):
    def one(dim, shards_of):
        steps = jax.random.uniform(jax.random.fold_in(jax.random.fold_in(stream_key, 6), dim), (shards_of,), jnp.float32, least / len(pieces), top_value / len(pieces))
        return jnp.repeat(jnp.exp(steps), shape[dim] // shards_of).reshape((-1,) + (1,) * (len(shape) - dim - 1))

    gain = one(*pieces[0])
    for cut in pieces[1:]:
        gain = gain * one(*cut)
    return gain


def bell_draw(key, dims, deviation, most, shards=(), kind=jnp.bfloat16):
    factor_of = levels(key, dims, shards, -0.22, 0.18) if shards else 1.0
    values = jax.random.normal(key, dims, jnp.float32) * deviation * factor_of
    return jnp.minimum(jnp.maximum(values, -most), most).astype(kind)


def noise_with(own_key, dims, spread, most, shards, heavy, dtype=jnp.bfloat16):
    array = spread * jax.random.normal(own_key, dims, jnp.float32)
    if shards:
        array = array * levels(own_key, dims, shards, -0.22, 0.18)
    return jnp.clip(raised(array, jax.random.fold_in(own_key, 3), *heavy), -most, most).astype(dtype)


def setup_inputs(seed: int = 0) -> dict:
    key_list = jax.random.split(jax.random.key(seed), 6)
    return {
        "inputs": bell_draw(key_list[0], (MB, TOKENS, D), 1.0, 6.0, ((1, 4),)),
        "cotangent": bell_draw(key_list[1], (MB, TOKENS, D), 1.0, 6.0, ((1, 4),)),
        "w_prev": bell_draw(key_list[2], (SECTIONS, D, D), 1.0, 6.0, ((0, 8), (2, 4)), jnp.float32),
        "w_now": bell_draw(key_list[3], (SECTIONS, D, D), 1.0, 6.0, ((0, 8), (2, 4)), jnp.float32),
        "grads_prev": noise_with(key_list[4], (N_DP, SECTIONS, D, D), 0.5, 6.0, ((0, 4), (1, 8)), (0, 3, 4, 2.0)),
    }


norm_eps = 1e-06
learn_rate = 1.0

def section_parts(x_bf, weight_bf):
    width = weight_bf.shape[0]
    inv = width ** (-0.5)
    x = x_bf.astype(jnp.float32)
    scale = lax.rsqrt(lax.optimization_barrier(jnp.mean(x * x, axis=-1, keepdims=True)) + norm_eps)
    normed = x * scale
    upper = normed.astype(jnp.bfloat16)
    pre = jnp.dot(upper.reshape(-1, width), weight_bf, preferred_element_type=jnp.float32).reshape(x.shape) * inv
    return (x, scale, normed, upper, pre)

def reference(inputs, cotangent, w_prev, w_now, grads_prev):
    n_rep = grads_prev.shape[0]
    sections = w_prev.shape[0]
    width = w_prev.shape[1]
    inv = width ** (-0.5)
    micro = inputs.shape[0]
    tok_mb = inputs.shape[1] // n_rep
    acts = inputs
    saved = []
    for s in range(sections):
        weight_bf = w_prev[s].astype(jnp.bfloat16)
        saved.append(acts)
        x, scale, normed, upper, pre = section_parts(acts, weight_bf)
        acts = (x + jax.nn.silu(pre)).astype(jnp.bfloat16)
    back = cotangent
    grads = [None] * sections
    for s in reversed(range(sections)):
        weight_bf = w_prev[s].astype(jnp.bfloat16)
        x, scale, normed, upper, pre = section_parts(saved[s], weight_bf)
        dy = back.astype(jnp.float32)
        sig = jax.nn.sigmoid(pre)
        dpre = dy * sig * (1.0 + pre * (1.0 - sig))
        small = (dpre * inv).astype(jnp.bfloat16)
        du = jnp.dot(small.reshape(-1, width), weight_bf.T, preferred_element_type=jnp.float32).reshape(x.shape)
        dx = dy + scale * (du - normed * lax.optimization_barrier(jnp.mean(du * normed, axis=-1, keepdims=True)))
        back = dx.astype(jnp.bfloat16)
        upper_r = upper.reshape(micro, n_rep, tok_mb, width).astype(jnp.float32)
        small_r = small.reshape(micro, n_rep, tok_mb, width).astype(jnp.float32)
        grads[s] = jnp.einsum('mrtd,mrte->rde', upper_r, small_r).astype(jnp.bfloat16)
    grads_next = jnp.stack(grads, axis=1)
    total = jnp.zeros(w_now.shape, jnp.float32)
    for rep in range(n_rep):
        total = total + grads_prev[rep].astype(jnp.float32)
    w_next = w_now - learn_rate * total / n_rep
    return (w_next, grads_next)
```

```python
import functools

import jax
import jax.numpy as jnp
from jax import lax
from jax.experimental import pallas as pl
from jax.experimental.pallas import tpu as pltpu
from jax.sharding import PartitionSpec as P

norm_eps = 1e-06
learn_rate = 1.0
MESH = pl.DeviceIdType.MESH
SPLIT = 2


def flipped(me, mask):
    out, bit, left = me, 1, mask
    while left:
        if left & 1:
            out = out + bit * (1 - 2 * ((me // bit) % 2))
        left >>= 1
        bit <<= 1
    return out


def spans(order):
    masks = [0]
    for bit in order:
        masks = masks + [mask ^ bit for mask in masks]
    return masks


def relay(n_rep, sections, chunk, x_hbm, cot_hbm, w_hbm, g_hbm,
          u_ref, q_ref, own_ref, far_ref,
          wf, weight, xin, dyin, ybuf, dxbuf, zbuf, rbuf, dubuf, local, part_sum, landed,
          tok, zout, load_sem, x_sem, cot_sem, local_sem,
          ag_send, ag_recv, rs_send, rs_recv, f_send, f_recv, b_send, b_recv,
          z_send, z_recv, gate, back):
    me = lax.axis_index("dp")
    sec = lax.axis_index("section")
    last = sections - 1
    rows, width = x_hbm.shape
    cols = width // n_rep
    half = width // 2
    n_chunks = rows // chunk
    inv = width ** (-0.5)
    bits = [1 << i for i in range(n_rep.bit_length() - 1)]
    orders = (bits, bits[::-1])

    for part in range(2):
        sl = pl.ds(part * half, half)
        copy = pltpu.make_async_copy(w_hbm.at[sl, :], wf.at[sl, :], load_sem.at[part])
        copy.start()

    def x_load(j):
        return pltpu.make_async_copy(
            x_hbm.at[:, pl.ds(j * cols, cols)], xin.at[j], x_sem.at[j])

    def cot_load(j):
        return pltpu.make_async_copy(
            cot_hbm.at[:, pl.ds(j * cols, cols)], dyin.at[j], cot_sem.at[j])

    @pl.when(sec == 0)
    def _():
        for j in range(n_rep):
            x_load(j).start()

    @pl.when(sec == last)
    def _():
        for j in range(n_rep):
            cot_load(j).start()

    def g_block(part, mask):
        at = pl.multiple_of(flipped(me, mask) * cols, cols)
        return g_hbm.at[pl.ds(part * half, half), pl.ds(at, cols)]

    barrier = pltpu.get_barrier_semaphore()
    for mask in range(1, n_rep):
        pl.semaphore_signal(barrier, inc=1, device_id={"dp": flipped(me, mask)}, device_id_type=MESH)

    @pl.when(sec > 0)
    def _():
        pl.semaphore_signal(barrier, inc=1, device_id={"section": sec - 1}, device_id_type=MESH)

    @pl.when(sec < last)
    def _():
        pl.semaphore_signal(barrier, inc=1, device_id={"section": sec + 1}, device_id_type=MESH)

    neighbours = (sec + last) // sections + (2 * last - sec) // sections
    pl.semaphore_wait(barrier, n_rep - 1 + neighbours)

    def piece_of(tokens, part, mask):
        if tokens:
            return tok.at[flipped(me, mask), pl.ds(part * (rows // 2), rows // 2), :]
        return weight.at[flipped(me, mask), pl.ds(part * half, half), :]

    def ag_copy(tokens, part, mask, bit):
        ref = piece_of(tokens, part, mask)
        return pltpu.make_async_remote_copy(
            src_ref=ref, dst_ref=ref,
            send_sem=ag_send.at[part, mask ^ bit], recv_sem=ag_recv.at[part, mask ^ bit],
            device_id={"dp": flipped(me, bit)}, device_id_type=MESH)

    def ag_arrival(tokens, part, mask):
        ref = piece_of(tokens, part, mask)
        return pltpu.make_async_remote_copy(
            src_ref=ref, dst_ref=ref,
            send_sem=ag_send.at[part, mask], recv_sem=ag_recv.at[part, mask],
            device_id={"dp": flipped(me, mask)}, device_id_type=MESH)

    def gather(tokens, prepare):
        for part in range(2):
            prepare(part)
            ag_copy(tokens, part, 0, orders[part][0]).start()
        for step in range(1, len(bits)):
            for part in range(2):
                ag_copy(tokens, part, 0, orders[part][step]).start()
        arrived = set()
        for step in range(1, len(bits)):
            for index in range(1, 1 << step):
                for part in range(2):
                    this = spans(orders[part][:step])[index]
                    if (part, this) not in arrived:
                        ag_arrival(tokens, part, this).wait_recv()
                        arrived.add((part, this))
                    ag_copy(tokens, part, this, orders[part][step]).start()
        return arrived

    def gather_sent(tokens):
        for part in range(2):
            for mask in range(1, n_rep):
                ag_copy(tokens, part, 0, mask).wait_send()

    def cast(part):
        pltpu.make_async_copy(
            w_hbm.at[pl.ds(part * half, half), :], wf.at[pl.ds(part * half, half), :],
            load_sem.at[part]).wait()
        piece = half // 4
        for i in range(4):
            sl = pl.ds(part * half + i * piece, piece)
            weight[me, sl, :] = wf[sl, :].astype(jnp.bfloat16)

    def normalise(sl):
        square = jnp.zeros((chunk, 1), jnp.float32)
        for j in range(n_rep):
            x = xin[j, sl, :].astype(jnp.float32)
            square += jnp.sum(x * x, axis=-1, keepdims=True)
        scale = lax.rsqrt(square * (1.0 / width) + norm_eps)
        rbuf[sl, :] = scale
        for j in range(n_rep):
            x = xin[j, sl, :].astype(jnp.float32)
            u_ref[sl, pl.ds(j * cols, cols)] = (x * scale).astype(jnp.bfloat16)

    def z_copy(part, mask):
        sl = pl.ds(part * (rows // 2), rows // 2)
        return pltpu.make_async_remote_copy(
            src_ref=zout.at[mask, sl, :], dst_ref=zbuf.at[me, sl, :],
            send_sem=z_send.at[part, mask], recv_sem=z_recv.at[part, mask],
            device_id={"dp": flipped(me, mask)}, device_id_type=MESH)

    def z_arrival(part, mask):
        sl = pl.ds(part * (rows // 2), rows // 2)
        return pltpu.make_async_remote_copy(
            src_ref=zout.at[mask, sl, :], dst_ref=zbuf.at[flipped(me, mask), sl, :],
            send_sem=z_send.at[part, mask], recv_sem=z_recv.at[part, mask],
            device_id={"dp": flipped(me, mask)}, device_id_type=MESH)

    odd = lax.rem(sec, 2) == 1

    @pl.when(sec == 0)
    def _():
        for j in range(n_rep):
            x_load(j).wait()

        def prepare(part):
            @pl.loop(part * (n_chunks // 2), (part + 1) * (n_chunks // 2))
            def _(c):
                sl = pl.ds(pl.multiple_of(c * chunk, chunk), chunk)
                normalise(sl)
                tok[me, sl, :] = u_ref[sl, :]

        arrived = gather(True, prepare)
        for part in range(2):
            cast(part)
        for mask in range(n_rep):
            for part in range(2):
                if mask and (part, mask) not in arrived:
                    ag_arrival(True, part, mask).wait_recv()
                sl = pl.ds(part * (rows // 2), rows // 2)
                z = jnp.dot(tok[flipped(me, mask), sl, :], weight[me],
                            preferred_element_type=jnp.float32) * inv
                if mask:
                    zout[mask, sl, :] = z
                    z_copy(part, mask).start()
                else:
                    zbuf[me, sl, :] = z
            if mask == 0:
                gather_sent(True)
                pl.semaphore_signal(
                    gate, inc=1, device_id={"section": sec + 1}, device_id_type=MESH)

    @pl.when((sec > 0) & jnp.logical_not(odd))
    def _():
        arrived = gather(False, cast)
        gather_sent(False)
        pl.semaphore_signal(
            gate, inc=1, device_id={"section": jnp.minimum(sec + 1, last)}, device_id_type=MESH)
        for part in range(2):
            for mask in range(1, n_rep):
                if (part, mask) not in arrived:
                    ag_arrival(False, part, mask).wait_recv()

    def rs_send_copy(part, step, mask, source):
        bit = orders[part][step]
        slot = mask ^ bit
        if step == len(bits) - 1:
            target = far_ref.at[pl.ds(part * half, half), :]
        else:
            target = landed.at[part, slot_of(part, step, slot)]
        return pltpu.make_async_remote_copy(
            src_ref=source, dst_ref=target,
            send_sem=rs_send.at[part, slot_of(part, step, slot)],
            recv_sem=rs_recv.at[part, slot_of(part, step, slot)],
            device_id={"dp": flipped(me, bit)}, device_id_type=MESH)

    def kept(part, step):
        return sorted(spans(orders[part][step:]))

    def slot_of(part, step, mask):
        base = sum(len(kept(part, s + 1)) for s in range(step))
        return base + kept(part, step + 1).index(mask)

    def local_copy(part, mask):
        at = kept(part, 1).index(mask)
        return pltpu.make_async_copy(
            g_block(part, mask), local.at[part, at], local_sem.at[part, at])

    def rs_start():
        for mask_at in range(n_rep // 2):
            for part in range(2):
                mask = kept(part, 1)[mask_at] ^ orders[part][0]
                rs_send_copy(part, 0, mask, g_block(part, mask)).start()
        for part in range(2):
            for mask in kept(part, 1):
                local_copy(part, mask).start()

    early = sections // 2

    @pl.when(odd)
    def _():
        pl.semaphore_wait(gate, 1)
        arrived = gather(False, cast)
        gather_sent(False)
        pl.semaphore_signal(
            back, inc=1, device_id={"section": jnp.maximum(sec - 1, 0)}, device_id_type=MESH)
        rs_start()
        for part in range(2):
            for mask in range(1, n_rep):
                if (part, mask) not in arrived:
                    ag_arrival(False, part, mask).wait_recv()

    @pl.when(jnp.logical_not(odd) & (sec >= early))
    def _():
        pl.semaphore_wait(back, 1)
        rs_start()

    def f_copy(c, j):
        sl = pl.ds(pl.multiple_of(c * chunk, chunk), chunk)
        return pltpu.make_async_remote_copy(
            src_ref=ybuf.at[j, sl, :], dst_ref=xin.at[j, sl, :],
            send_sem=f_send.at[c, j], recv_sem=f_recv.at[c, j],
            device_id={"section": jnp.minimum(sec + 1, last)}, device_id_type=MESH)

    def b_copy(c, j):
        sl = pl.ds(pl.multiple_of(c * chunk, chunk), chunk)
        return pltpu.make_async_remote_copy(
            src_ref=dxbuf.at[j, sl, :], dst_ref=dyin.at[j, sl, :],
            send_sem=b_send.at[c, j], recv_sem=b_recv.at[c, j],
            device_id={"section": jnp.maximum(sec - 1, 0)}, device_id_type=MESH)

    @pl.when(sec == 0)
    def _():
        for part in range(2):
            for mask in range(1, n_rep):
                z_arrival(part, mask).wait_recv()

    @pl.when(sec == last)
    def _():
        for j in range(n_rep):
            cot_load(j).wait()

    @pl.loop(0, n_chunks)
    def _(c):
        sl = pl.ds(pl.multiple_of(c * chunk, chunk), chunk)

        @pl.when(sec > 0)
        def _():
            for j in range(n_rep):
                f_copy(c, j).wait_recv()
            normalise(sl)

        for j in range(n_rep):
            @pl.when(sec > 0)
            def _():
                zbuf[j, sl, :] = jnp.dot(
                    u_ref[sl, :], weight[j], preferred_element_type=jnp.float32) * inv

            @pl.when(sec < last)
            def _():
                zz = zbuf[j, sl, :]
                y = xin[j, sl, :].astype(jnp.float32) + zz * jax.nn.sigmoid(zz)
                ybuf[j, sl, :] = y.astype(jnp.bfloat16)
                f_copy(c, j).start()

    def rs_middle():
        for step in range(1, len(bits)):
            for part in range(2):
                for mask in kept(part, step):
                    rs_send_copy(part, step - 1, mask ^ orders[part][step - 1],
                                 landed.at[part, 0]).wait_recv()
                    at = kept(part, 1).index(mask)
                    if step == 1:
                        local_copy(part, mask).wait()
                    pieces = 4
                    piece = half // pieces
                    for i in range(pieces):
                        ps = pl.ds(i * piece, piece)
                        if step == 1:
                            mine = local[part, at, ps, :].astype(jnp.float32)
                        elif mask:
                            mine = part_sum[part, at, ps, :].astype(jnp.float32)
                        else:
                            mine = own_ref[pl.ds(part * half + i * piece, piece), :].astype(jnp.float32)
                        total = mine + landed[part, slot_of(part, step - 1, mask), ps, :].astype(jnp.float32)
                        total = total.astype(jnp.bfloat16)
                        if mask:
                            part_sum[part, at, ps, :] = total
                        else:
                            own_ref[pl.ds(part * half + i * piece, piece), :] = total
                    if mask & orders[part][step]:
                        rs_send_copy(part, step, mask, part_sum.at[part, at]).start()

    @pl.when(jnp.logical_not(odd) & (sec < early))
    def _():
        pl.semaphore_wait(back, 1)
        rs_start()

    @pl.when(sec < early)
    def _():
        rs_middle()

    @pl.loop(0, n_chunks)
    def _(c):
        sl = pl.ds(pl.multiple_of(c * chunk, chunk), chunk)
        for j in range(n_rep):
            @pl.when(sec < last)
            def _():
                b_copy(c, j).wait_recv()

            z = zbuf[j, sl, :]
            sig = jax.nn.sigmoid(z)
            dz = dyin[j, sl, :].astype(jnp.float32) * sig * (1.0 + z * (1.0 - sig))
            q_ref[sl, pl.ds(j * cols, cols)] = (dz * inv).astype(jnp.bfloat16)

            @pl.when(sec > 0)
            def _():
                q = q_ref[sl, pl.ds(j * cols, cols)]
                for k in range(n_rep):
                    du = lax.dot_general(
                        q, weight[j, pl.ds(k * cols, cols), :],
                        (((1,), (1,)), ((), ())), preferred_element_type=jnp.float32)
                    dubuf[k] = du if j == 0 else dubuf[k] + du

        @pl.when(sec > 0)
        def _():
            scale = rbuf[sl, :]
            dot_sum = jnp.zeros((chunk, 1), jnp.float32)
            for k in range(n_rep):
                normed = xin[k, sl, :].astype(jnp.float32) * scale
                dot_sum += jnp.sum(dubuf[k] * normed, axis=-1, keepdims=True)
            mean = dot_sum * (1.0 / width)
            for k in range(n_rep):
                normed = xin[k, sl, :].astype(jnp.float32) * scale
                dx = dyin[k, sl, :].astype(jnp.float32) + scale * (dubuf[k] - normed * mean)
                dxbuf[k, sl, :] = dx.astype(jnp.bfloat16)
                b_copy(c, k).start()

    @pl.when(sec >= early)
    def _():
        rs_middle()

    final = len(bits) - 1
    for part in range(2):
        rs_send_copy(part, final, orders[part][final], part_sum.at[part, 0]).wait_recv()
    @pl.when(sec == 0)
    def _():
        for part in range(2):
            for mask in range(1, n_rep):
                z_copy(part, mask).wait_send()

    for part in range(2):
        for step in range(len(bits)):
            for mask in kept(part, step + 1):
                rs_send_copy(part, step, mask ^ orders[part][step], part_sum.at[part, 0]).wait_send()

    @pl.when(sec < last)
    def _():
        @pl.loop(0, n_chunks)
        def _(c):
            for j in range(n_rep):
                f_copy(c, j).wait_send()

    @pl.when(sec > 0)
    def _():
        @pl.loop(0, n_chunks)
        def _(c):
            for j in range(n_rep):
                b_copy(c, j).wait_send()


def finish(rate, u_hbm, q_hbm, own_hbm, far_hbm, now_hbm, next_hbm, grad_hbm,
           u_ref, q_ref, own_ref, far_ref, now_ref, next_ref, grad_ref, act_sem, in_sem, next_sem, grad_sem):
    tile = next_ref.shape[1]
    count = next_ref.shape[0]

    def act_load(i):
        source, target = ((u_hbm, u_ref), (q_hbm, q_ref))[i]
        return pltpu.make_async_copy(source, target, act_sem.at[i])

    def loads(t):
        rows = pl.ds(t * tile, tile)
        pairs = ((own_hbm, own_ref), (far_hbm, far_ref), (now_hbm, now_ref))
        return [pltpu.make_async_copy(source.at[rows, :], target.at[t], in_sem.at[i, t])
                for i, (source, target) in enumerate(pairs)]

    def next_store(t):
        return pltpu.make_async_copy(
            next_ref.at[t], next_hbm.at[pl.ds(t * tile, tile), :], next_sem.at[t])

    def grad_store(t):
        return pltpu.make_async_copy(
            grad_ref.at[t], grad_hbm.at[pl.ds(t * tile, tile), :], grad_sem.at[t])

    for i in range(2):
        act_load(i).start()
    for t in range(count):
        for copy in loads(t):
            copy.start()
    for i in range(2):
        act_load(i).wait()
    for t in range(count):
        grad_ref[t] = lax.dot_general(
            u_ref[:, pl.ds(t * tile, tile)], q_ref[...], (((0,), (0,)), ((), ())),
            preferred_element_type=jnp.float32).astype(jnp.bfloat16)
        grad_store(t).start()
        for copy in loads(t):
            copy.wait()
        total = own_ref[t].astype(jnp.float32) + far_ref[t].astype(jnp.float32)
        next_ref[t] = now_ref[t] - rate * total
        next_store(t).start()
    for t in range(count):
        grad_store(t).wait()
        next_store(t).wait()


def body(inputs, cotangent, w_prev, w_now, grads_prev):
    sections = lax.axis_size("section")
    n_rep = lax.axis_size("dp")
    micro, tok_mb, width = inputs.shape
    rows = micro * tok_mb
    cols = width // n_rep
    half = width // 2
    chunk = tok_mb // SPLIT
    n_chunks = rows // chunk
    any_spec = pl.BlockSpec(memory_space=pl.ANY)
    vmem_spec = pl.BlockSpec(memory_space=pltpu.VMEM)
    bf16, f32 = jnp.bfloat16, jnp.float32
    dma = pltpu.SemaphoreType.DMA
    upper, small, own, far = pl.pallas_call(
        functools.partial(relay, n_rep, sections, chunk),
        out_shape=(
            jax.ShapeDtypeStruct((rows, width), bf16),
            jax.ShapeDtypeStruct((rows, width), bf16),
            jax.ShapeDtypeStruct((width, cols), bf16),
            jax.ShapeDtypeStruct((width, cols), bf16),
        ),
        in_specs=[any_spec] * 4,
        out_specs=(vmem_spec,) * 4,
        scratch_shapes=[
            pltpu.VMEM((width, cols), f32),
            pltpu.VMEM((n_rep, width, cols), bf16),
            pltpu.VMEM((n_rep, rows, cols), bf16),
            pltpu.VMEM((n_rep, rows, cols), bf16),
            pltpu.VMEM((n_rep, rows, cols), bf16),
            pltpu.VMEM((n_rep, rows, cols), bf16),
            pltpu.VMEM((n_rep, rows, cols), f32),
            pltpu.VMEM((rows, 1), f32),
            pltpu.VMEM((n_rep, chunk, cols), f32),
            pltpu.VMEM((2, n_rep // 2, half, cols), bf16),
            pltpu.VMEM((2, n_rep // 2, half, cols), bf16),
            pltpu.VMEM((2, max(1, n_rep - 2), half, cols), bf16),
            pltpu.VMEM((n_rep, rows, width), bf16),
            pltpu.VMEM((n_rep, rows, cols), f32),
            dma((2,)), dma((n_rep,)), dma((n_rep,)), dma((2, n_rep // 2)),
            dma((2, n_rep)), dma((2, n_rep)),
            dma((2, n_rep)), dma((2, n_rep)),
            dma((n_chunks, n_rep)), dma((n_chunks, n_rep)),
            dma((n_chunks, n_rep)), dma((n_chunks, n_rep)),
            dma((2, n_rep)), dma((2, n_rep)),
            pltpu.SemaphoreType.REGULAR, pltpu.SemaphoreType.REGULAR,
        ],
        compiler_params=pltpu.CompilerParams(
            collective_id=0, has_side_effects=True, vmem_limit_bytes=60 * 1024 * 1024
        ),
        name="relay",
    )(inputs.reshape(rows, width), cotangent.reshape(rows, width), w_prev[0], grads_prev[0, 0])
    count = 8
    tile = width // count
    w_next, grads_next = pl.pallas_call(
        functools.partial(finish, learn_rate / n_rep),
        out_shape=(
            jax.ShapeDtypeStruct((width, cols), f32),
            jax.ShapeDtypeStruct((width, width), bf16),
        ),
        in_specs=[any_spec] * 5,
        out_specs=(any_spec,) * 2,
        scratch_shapes=[
            pltpu.VMEM((rows, width), bf16),
            pltpu.VMEM((rows, width), bf16),
            pltpu.VMEM((count, tile, cols), bf16),
            pltpu.VMEM((count, tile, cols), bf16),
            pltpu.VMEM((count, tile, cols), f32),
            pltpu.VMEM((count, tile, cols), f32),
            pltpu.VMEM((count, tile, width), bf16),
            dma((2,)), dma((3, count)), dma((count,)), dma((count,)),
        ],
        compiler_params=pltpu.CompilerParams(vmem_limit_bytes=40 * 1024 * 1024),
        name="finish",
    )(upper, small, own, far, w_now[0])
    return (w_next[None], grads_next[None, None])


def solution(mesh):
    return jax.shard_map(
        body,
        mesh=mesh,
        in_specs=(
            P(None, "dp", None),
            P(None, "dp", None),
            P("section", None, "dp"),
            P("section", None, "dp"),
            P("dp", "section", None, None),
        ),
        out_specs=(P("section", None, "dp"), P("dp", "section", None, None)),
        check_vma=False,
    )
```

```python
import functools

import jax
import jax.numpy as jnp
from jax import lax
from jax.experimental import pallas as pl
from jax.experimental.pallas import tpu as pltpu
from jax.sharding import PartitionSpec as P

norm_eps = 1e-06
learn_rate = 1.0
MESH = pl.DeviceIdType.MESH
SPLIT = 2


def flipped(me, mask):
    out, bit, left = me, 1, mask
    while left:
        if left & 1:
            out = out + bit * (1 - 2 * ((me // bit) % 2))
        left >>= 1
        bit <<= 1
    return out


def spans(order):
    masks = [0]
    for bit in order:
        masks = masks + [mask ^ bit for mask in masks]
    return masks


def relay(n_rep, sections, chunk, x_hbm, cot_hbm, w_hbm, g_hbm,
          u_ref, q_ref, own_ref, far_ref,
          wf, weight, turned, xin, dyin, ybuf, dxbuf, zbuf, rbuf, dubuf, local, part_sum, landed,
          tok, zout, zland, load_sem, x_sem, cot_sem, local_sem,
          ag_send, ag_recv, rs_send, rs_recv, f_send, f_recv, b_send, b_recv,
          z_send, z_recv, gate, back):
    me = lax.axis_index("dp")
    sec = lax.axis_index("section")
    last = sections - 1
    rows, width = x_hbm.shape
    cols = width // n_rep
    half = width // 2
    n_chunks = rows // chunk
    inv = width ** (-0.5)
    bits = [1 << i for i in range(n_rep.bit_length() - 1)]
    orders = (bits, bits[::-1])

    for part in range(2):
        sl = pl.ds(part * half, half)
        copy = pltpu.make_async_copy(w_hbm.at[sl, :], wf.at[sl, :], load_sem.at[part])
        copy.start()

    def x_load(j):
        return pltpu.make_async_copy(
            x_hbm.at[:, pl.ds(j * cols, cols)], xin.at[j], x_sem.at[j])

    def cot_load(j):
        return pltpu.make_async_copy(
            cot_hbm.at[:, pl.ds(j * cols, cols)], dyin.at[j], cot_sem.at[j])

    @pl.when(sec == 0)
    def _():
        for j in range(n_rep):
            x_load(j).start()

    @pl.when(sec == last)
    def _():
        for j in range(n_rep):
            cot_load(j).start()

    def g_block(part, mask):
        at = pl.multiple_of(flipped(me, mask) * cols, cols)
        return g_hbm.at[pl.ds(part * half, half), pl.ds(at, cols)]

    barrier = pltpu.get_barrier_semaphore()
    for mask in range(1, n_rep):
        pl.semaphore_signal(barrier, inc=1, device_id={"dp": flipped(me, mask)}, device_id_type=MESH)

    @pl.when(sec > 0)
    def _():
        pl.semaphore_signal(barrier, inc=1, device_id={"section": sec - 1}, device_id_type=MESH)

    @pl.when(sec < last)
    def _():
        pl.semaphore_signal(barrier, inc=1, device_id={"section": sec + 1}, device_id_type=MESH)

    neighbours = (sec + last) // sections + (2 * last - sec) // sections
    pl.semaphore_wait(barrier, n_rep - 1 + neighbours)

    def piece_of(tokens, part, mask):
        if tokens:
            return tok.at[flipped(me, mask), pl.ds(part * (rows // 2), rows // 2), :]
        return weight.at[flipped(me, mask), pl.ds(part * half, half), :]

    def ag_copy(tokens, part, mask, bit):
        ref = piece_of(tokens, part, mask)
        return pltpu.make_async_remote_copy(
            src_ref=ref, dst_ref=ref,
            send_sem=ag_send.at[part, mask ^ bit], recv_sem=ag_recv.at[part, mask ^ bit],
            device_id={"dp": flipped(me, bit)}, device_id_type=MESH)

    def ag_arrival(tokens, part, mask):
        ref = piece_of(tokens, part, mask)
        return pltpu.make_async_remote_copy(
            src_ref=ref, dst_ref=ref,
            send_sem=ag_send.at[part, mask], recv_sem=ag_recv.at[part, mask],
            device_id={"dp": flipped(me, mask)}, device_id_type=MESH)

    def gather(tokens, prepare):
        for part in range(2):
            prepare(part)
            ag_copy(tokens, part, 0, orders[part][0]).start()
        for step in range(1, len(bits)):
            for part in range(2):
                ag_copy(tokens, part, 0, orders[part][step]).start()
        arrived = set()
        for step in range(1, len(bits)):
            for index in range(1, 1 << step):
                for part in range(2):
                    this = spans(orders[part][:step])[index]
                    if (part, this) not in arrived:
                        ag_arrival(tokens, part, this).wait_recv()
                        arrived.add((part, this))
                    ag_copy(tokens, part, this, orders[part][step]).start()
        return arrived

    def gather_sent(tokens, masks):
        for part in range(2):
            for mask in masks:
                ag_copy(tokens, part, 0, mask).wait_send()

    everyone = range(1, n_rep)
    relayed = [mask for mask in everyone if mask not in bits]

    def cast(part):
        pltpu.make_async_copy(
            w_hbm.at[pl.ds(part * half, half), :], wf.at[pl.ds(part * half, half), :],
            load_sem.at[part]).wait()
        piece = half // 4
        for i in range(4):
            sl = pl.ds(part * half + i * piece, piece)
            weight[me, sl, :] = wf[sl, :].astype(jnp.bfloat16)

    def normalise(sl):
        square = jnp.zeros((chunk, 1), jnp.float32)
        for j in range(n_rep):
            x = xin[j, sl, :].astype(jnp.float32)
            square += jnp.sum(x * x, axis=-1, keepdims=True)
        scale = lax.rsqrt(square * (1.0 / width) + norm_eps)
        rbuf[sl, :] = scale
        for j in range(n_rep):
            x = xin[j, sl, :].astype(jnp.float32)
            u_ref[sl, pl.ds(j * cols, cols)] = (x * scale).astype(jnp.bfloat16)

    def z_copy(part, mask):
        sl = pl.ds(part * (rows // 2), rows // 2)
        return pltpu.make_async_remote_copy(
            src_ref=zout.at[mask, sl, :], dst_ref=zland.at[me, sl, :],
            send_sem=z_send.at[part, mask], recv_sem=z_recv.at[part, mask],
            device_id={"dp": flipped(me, mask)}, device_id_type=MESH)

    def z_arrival(part, mask):
        sl = pl.ds(part * (rows // 2), rows // 2)
        return pltpu.make_async_remote_copy(
            src_ref=zout.at[mask, sl, :], dst_ref=zland.at[flipped(me, mask), sl, :],
            send_sem=z_send.at[part, mask], recv_sem=z_recv.at[part, mask],
            device_id={"dp": flipped(me, mask)}, device_id_type=MESH)

    odd = lax.rem(sec, 2) == 1

    def turn():
        @pl.loop(0, n_rep)
        def _(j):
            for k in range(n_rep):
                span = pl.ds(k * cols, cols)
                turned[j, :, span] = weight[j, span, :].T

    @pl.when(sec == 0)
    def _():
        for j in range(n_rep):
            x_load(j).wait()

        def prepare(part):
            @pl.loop(part * (n_chunks // 2), (part + 1) * (n_chunks // 2))
            def _(c):
                sl = pl.ds(pl.multiple_of(c * chunk, chunk), chunk)
                normalise(sl)
                tok[me, sl, :] = u_ref[sl, :]

        arrived = gather(True, prepare)
        for part in range(2):
            cast(part)
        for mask in range(n_rep):
            for part in range(2):
                if mask and (part, mask) not in arrived:
                    ag_arrival(True, part, mask).wait_recv()
                sl = pl.ds(part * (rows // 2), rows // 2)
                z = jnp.dot(tok[flipped(me, mask), sl, :], weight[me],
                            preferred_element_type=jnp.float32) * inv
                if mask:
                    zout[mask, sl, :] = z.astype(jnp.bfloat16)
                    z_copy(part, mask).start()
                else:
                    zbuf[me, sl, :] = z
        gather_sent(True, everyone)

    @pl.when((sec > 0) & jnp.logical_not(odd))
    def _():
        arrived = gather(False, cast)
        gather_sent(False, bits)
        pl.semaphore_signal(
            gate, inc=1, device_id={"section": jnp.minimum(sec + 1, last)}, device_id_type=MESH)
        gather_sent(False, relayed)
        for part in range(2):
            for mask in range(1, n_rep):
                if (part, mask) not in arrived:
                    ag_arrival(False, part, mask).wait_recv()
        turn()

    def rs_send_copy(part, step, mask, source):
        bit = orders[part][step]
        slot = mask ^ bit
        if step == len(bits) - 1:
            target = far_ref.at[pl.ds(part * half, half), :]
        else:
            target = landed.at[part, slot_of(part, step, slot)]
        return pltpu.make_async_remote_copy(
            src_ref=source, dst_ref=target,
            send_sem=rs_send.at[part, slot_of(part, step, slot)],
            recv_sem=rs_recv.at[part, slot_of(part, step, slot)],
            device_id={"dp": flipped(me, bit)}, device_id_type=MESH)

    def kept(part, step):
        return sorted(spans(orders[part][step:]))

    def ordered(part, step):
        return sorted(kept(part, step), key=lambda mask: (not mask & orders[part][step], mask))

    def slot_of(part, step, mask):
        base = sum(len(kept(part, s + 1)) for s in range(step))
        return base + kept(part, step + 1).index(mask)

    def local_copy(part, mask):
        at = kept(part, 1).index(mask)
        return pltpu.make_async_copy(
            g_block(part, mask), local.at[part, at], local_sem.at[part, at])

    def rs_start():
        for mask_at in range(n_rep // 2):
            for part in range(2):
                mask = ordered(part, 1)[mask_at] ^ orders[part][0]
                rs_send_copy(part, 0, mask, g_block(part, mask)).start()
        for part in range(2):
            for mask in ordered(part, 1):
                local_copy(part, mask).start()

    early = sections // 2

    @pl.when(odd)
    def _():
        @pl.when(sec > 1)
        def _():
            pl.semaphore_wait(gate, 1)

        arrived = gather(False, cast)
        gather_sent(False, everyone)
        pl.semaphore_signal(
            back, inc=1, device_id={"section": jnp.maximum(sec - 1, 0)}, device_id_type=MESH)
        rs_start()
        for part in range(2):
            for mask in range(1, n_rep):
                if (part, mask) not in arrived:
                    ag_arrival(False, part, mask).wait_recv()

    @pl.when(odd & (sec >= early))
    def _():
        turn()

    @pl.when(jnp.logical_not(odd) & (sec >= early))
    def _():
        pl.semaphore_wait(back, 1)
        rs_start()

    def f_copy(c, j):
        sl = pl.ds(pl.multiple_of(c * chunk, chunk), chunk)
        return pltpu.make_async_remote_copy(
            src_ref=ybuf.at[j, sl, :], dst_ref=xin.at[j, sl, :],
            send_sem=f_send.at[c, j], recv_sem=f_recv.at[c, j],
            device_id={"section": jnp.minimum(sec + 1, last)}, device_id_type=MESH)

    def b_copy(c, j):
        sl = pl.ds(pl.multiple_of(c * chunk, chunk), chunk)
        return pltpu.make_async_remote_copy(
            src_ref=dxbuf.at[j, sl, :], dst_ref=dyin.at[j, sl, :],
            send_sem=b_send.at[c, j], recv_sem=b_recv.at[c, j],
            device_id={"section": jnp.maximum(sec - 1, 0)}, device_id_type=MESH)

    @pl.when(sec == 0)
    def _():
        for part in range(2):
            for mask in range(1, n_rep):
                z_arrival(part, mask).wait_recv()
                sl = pl.ds(part * (rows // 2), rows // 2)
                zbuf[flipped(me, mask), sl, :] = zland[flipped(me, mask), sl, :].astype(jnp.float32)

    @pl.when(sec == last)
    def _():
        for j in range(n_rep):
            cot_load(j).wait()

    def section_input(c):
        for j in range(n_rep):
            f_copy(c, j).wait_recv()
        normalise(pl.ds(pl.multiple_of(c * chunk, chunk), chunk))

    def project(c, j):
        sl = pl.ds(pl.multiple_of(c * chunk, chunk), chunk)
        zbuf[j, sl, :] = jnp.dot(
            u_ref[sl, :], weight[j], preferred_element_type=jnp.float32) * inv

    def emit(c, j):
        sl = pl.ds(pl.multiple_of(c * chunk, chunk), chunk)
        zz = zbuf[j, sl, :]
        y = xin[j, sl, :].astype(jnp.float32) + zz * jax.nn.sigmoid(zz)
        ybuf[j, sl, :] = y.astype(jnp.bfloat16)
        f_copy(c, j).start()

    def small_grad(c, j):
        sl = pl.ds(pl.multiple_of(c * chunk, chunk), chunk)
        z = zbuf[j, sl, :]
        sig = jax.nn.sigmoid(z)
        dz = dyin[j, sl, :].astype(jnp.float32) * sig * (1.0 + z * (1.0 - sig))
        q_ref[sl, pl.ds(j * cols, cols)] = (dz * inv).astype(jnp.bfloat16)

    def back_project(c, j):
        sl = pl.ds(pl.multiple_of(c * chunk, chunk), chunk)
        q = q_ref[sl, pl.ds(j * cols, cols)]
        for k in range(n_rep):
            du = jnp.dot(q, turned[j, :, pl.ds(k * cols, cols)], preferred_element_type=jnp.float32)
            dubuf[k] = du if j == 0 else dubuf[k] + du

    def emit_back(c):
        sl = pl.ds(pl.multiple_of(c * chunk, chunk), chunk)
        scale = rbuf[sl, :]
        dot_sum = jnp.zeros((chunk, 1), jnp.float32)
        for k in range(n_rep):
            normed = xin[k, sl, :].astype(jnp.float32) * scale
            dot_sum += jnp.sum(dubuf[k] * normed, axis=-1, keepdims=True)
        mean = dot_sum * (1.0 / width)
        for k in range(n_rep):
            normed = xin[k, sl, :].astype(jnp.float32) * scale
            dx = dyin[k, sl, :].astype(jnp.float32) + scale * (dubuf[k] - normed * mean)
            dxbuf[k, sl, :] = dx.astype(jnp.bfloat16)
            b_copy(c, k).start()

    middle = (sec > 0) & (sec < last)

    @pl.when(sec == 0)
    def _():
        @pl.loop(0, n_chunks)
        def _(c):
            for j in range(n_rep):
                emit(c, j)

    @pl.when(middle)
    def _():
        @pl.loop(0, n_chunks)
        def _(c):
            section_input(c)
            for j in range(n_rep):
                project(c, j)
                emit(c, j)

    def rs_add(step, part, mask):
        rs_send_copy(part, step - 1, mask ^ orders[part][step - 1],
                     landed.at[part, 0]).wait_recv()
        at = kept(part, 1).index(mask)
        if step == 1:
            local_copy(part, mask).wait()
        pieces = 4
        piece = half // pieces
        for i in range(pieces):
            ps = pl.ds(i * piece, piece)
            if step == 1:
                mine = local[part, at, ps, :].astype(jnp.float32)
            elif mask:
                mine = part_sum[part, at, ps, :].astype(jnp.float32)
            else:
                mine = own_ref[pl.ds(part * half + i * piece, piece), :].astype(jnp.float32)
            total = mine + landed[part, slot_of(part, step - 1, mask), ps, :].astype(jnp.float32)
            total = total.astype(jnp.bfloat16)
            if mask:
                part_sum[part, at, ps, :] = total
            else:
                own_ref[pl.ds(part * half + i * piece, piece), :] = total
        if mask & orders[part][step]:
            rs_send_copy(part, step, mask, part_sum.at[part, at]).start()

    def rs_middle(first):
        for step in range(1, len(bits)):
            for index in range(len(kept(0, step))):
                for part in range(2):
                    mask = ordered(part, step)[index]
                    if first == (step == 1 and mask & orders[part][1] > 0):
                        rs_add(step, part, mask)

    @pl.when(odd & (sec < early))
    def _():
        turn()

    @pl.when(jnp.logical_not(odd) & (sec < early))
    def _():
        pl.semaphore_wait(back, 1)
        rs_start()

    late = sections - 2

    @pl.when(sec < late)
    def _():
        rs_middle(True)

    @pl.when(sec < early)
    def _():
        rs_middle(False)

    @pl.when(sec == 0)
    def _():
        @pl.loop(0, n_chunks)
        def _(c):
            for j in range(n_rep):
                b_copy(c, j).wait_recv()
                small_grad(c, j)

    @pl.when(middle)
    def _():
        @pl.loop(0, n_chunks)
        def _(c):
            for j in range(n_rep):
                b_copy(c, j).wait_recv()
                small_grad(c, j)
                back_project(c, j)
            emit_back(c)

    @pl.when(sec == last)
    def _():
        @pl.loop(0, n_chunks)
        def _(c):
            section_input(c)
            for j in range(n_rep):
                project(c, j)
            for j in range(n_rep):
                small_grad(c, j)
                back_project(c, j)
            emit_back(c)

    @pl.when(sec >= late)
    def _():
        rs_middle(True)

    @pl.when(sec >= early)
    def _():
        rs_middle(False)

    final = len(bits) - 1
    for part in range(2):
        rs_send_copy(part, final, orders[part][final], part_sum.at[part, 0]).wait_recv()
    @pl.when(sec == 0)
    def _():
        for part in range(2):
            for mask in range(1, n_rep):
                z_copy(part, mask).wait_send()

    for part in range(2):
        for step in range(len(bits)):
            for mask in kept(part, step + 1):
                rs_send_copy(part, step, mask ^ orders[part][step], part_sum.at[part, 0]).wait_send()

    @pl.when(sec < last)
    def _():
        @pl.loop(0, n_chunks)
        def _(c):
            for j in range(n_rep):
                f_copy(c, j).wait_send()

    @pl.when(sec > 0)
    def _():
        @pl.loop(0, n_chunks)
        def _(c):
            for j in range(n_rep):
                b_copy(c, j).wait_send()


def finish(rate, u_hbm, q_hbm, own_hbm, far_hbm, now_hbm, next_hbm, grad_hbm,
           u_ref, q_ref, own_ref, far_ref, now_ref, next_ref, grad_ref, act_sem, in_sem, next_sem, grad_sem):
    tile = next_ref.shape[1]
    count = next_ref.shape[0]

    def act_load(i):
        source, target = ((u_hbm, u_ref), (q_hbm, q_ref))[i]
        return pltpu.make_async_copy(source, target, act_sem.at[i])

    def loads(t):
        rows = pl.ds(t * tile, tile)
        pairs = ((own_hbm, own_ref), (far_hbm, far_ref), (now_hbm, now_ref))
        return [pltpu.make_async_copy(source.at[rows, :], target.at[t], in_sem.at[i, t])
                for i, (source, target) in enumerate(pairs)]

    def next_store(t):
        return pltpu.make_async_copy(
            next_ref.at[t], next_hbm.at[pl.ds(t * tile, tile), :], next_sem.at[t])

    def grad_store(t):
        return pltpu.make_async_copy(
            grad_ref.at[t], grad_hbm.at[pl.ds(t * tile, tile), :], grad_sem.at[t])

    for i in range(2):
        act_load(i).start()
    for t in range(count):
        for copy in loads(t):
            copy.start()
    for i in range(2):
        act_load(i).wait()
    for t in range(count):
        grad_ref[t] = lax.dot_general(
            u_ref[:, pl.ds(t * tile, tile)], q_ref[...], (((0,), (0,)), ((), ())),
            preferred_element_type=jnp.float32).astype(jnp.bfloat16)
        grad_store(t).start()
        for copy in loads(t):
            copy.wait()
        total = own_ref[t].astype(jnp.float32) + far_ref[t].astype(jnp.float32)
        next_ref[t] = now_ref[t] - rate * total
        next_store(t).start()
    for t in range(count):
        grad_store(t).wait()
        next_store(t).wait()


def body(inputs, cotangent, w_prev, w_now, grads_prev):
    sections = lax.axis_size("section")
    n_rep = lax.axis_size("dp")
    micro, tok_mb, width = inputs.shape
    rows = micro * tok_mb
    cols = width // n_rep
    half = width // 2
    chunk = tok_mb // SPLIT
    n_chunks = rows // chunk
    any_spec = pl.BlockSpec(memory_space=pl.ANY)
    vmem_spec = pl.BlockSpec(memory_space=pltpu.VMEM)
    bf16, f32 = jnp.bfloat16, jnp.float32
    dma = pltpu.SemaphoreType.DMA
    upper, small, own, far = pl.pallas_call(
        functools.partial(relay, n_rep, sections, chunk),
        out_shape=(
            jax.ShapeDtypeStruct((rows, width), bf16),
            jax.ShapeDtypeStruct((rows, width), bf16),
            jax.ShapeDtypeStruct((width, cols), bf16),
            jax.ShapeDtypeStruct((width, cols), bf16),
        ),
        in_specs=[any_spec] * 4,
        out_specs=(vmem_spec,) * 4,
        scratch_shapes=[
            pltpu.VMEM((width, cols), f32),
            pltpu.VMEM((n_rep, width, cols), bf16),
            pltpu.VMEM((n_rep, cols, width), bf16),
            pltpu.VMEM((n_rep, rows, cols), bf16),
            pltpu.VMEM((n_rep, rows, cols), bf16),
            pltpu.VMEM((n_rep, rows, cols), bf16),
            pltpu.VMEM((n_rep, rows, cols), bf16),
            pltpu.VMEM((n_rep, rows, cols), f32),
            pltpu.VMEM((rows, 1), f32),
            pltpu.VMEM((n_rep, chunk, cols), f32),
            pltpu.VMEM((2, n_rep // 2, half, cols), bf16),
            pltpu.VMEM((2, n_rep // 2, half, cols), bf16),
            pltpu.VMEM((2, max(1, n_rep - 2), half, cols), bf16),
            pltpu.VMEM((n_rep, rows, width), bf16),
            pltpu.VMEM((n_rep, rows, cols), bf16),
            pltpu.VMEM((n_rep, rows, cols), bf16),
            dma((2,)), dma((n_rep,)), dma((n_rep,)), dma((2, n_rep // 2)),
            dma((2, n_rep)), dma((2, n_rep)),
            dma((2, n_rep)), dma((2, n_rep)),
            dma((n_chunks, n_rep)), dma((n_chunks, n_rep)),
            dma((n_chunks, n_rep)), dma((n_chunks, n_rep)),
            dma((2, n_rep)), dma((2, n_rep)),
            pltpu.SemaphoreType.REGULAR, pltpu.SemaphoreType.REGULAR,
        ],
        compiler_params=pltpu.CompilerParams(
            collective_id=0, has_side_effects=True, vmem_limit_bytes=60 * 1024 * 1024
        ),
        name="relay",
    )(inputs.reshape(rows, width), cotangent.reshape(rows, width), w_prev[0], grads_prev[0, 0])
    count = 8
    tile = width // count
    w_next, grads_next = pl.pallas_call(
        functools.partial(finish, learn_rate / n_rep),
        out_shape=(
            jax.ShapeDtypeStruct((width, cols), f32),
            jax.ShapeDtypeStruct((width, width), bf16),
        ),
        in_specs=[any_spec] * 5,
        out_specs=(any_spec,) * 2,
        scratch_shapes=[
            pltpu.VMEM((rows, width), bf16),
            pltpu.VMEM((rows, width), bf16),
            pltpu.VMEM((count, tile, cols), bf16),
            pltpu.VMEM((count, tile, cols), bf16),
            pltpu.VMEM((count, tile, cols), f32),
            pltpu.VMEM((count, tile, cols), f32),
            pltpu.VMEM((count, tile, width), bf16),
            dma((2,)), dma((3, count)), dma((count,)), dma((count,)),
        ],
        compiler_params=pltpu.CompilerParams(vmem_limit_bytes=60 * 1024 * 1024),
        name="finish",
    )(upper, small, own, far, w_now[0])
    return (w_next[None], grads_next[None, None])


def solution(mesh):
    return jax.shard_map(
        body,
        mesh=mesh,
        in_specs=(
            P(None, "dp", None),
            P(None, "dp", None),
            P("section", None, "dp"),
            P("section", None, "dp"),
            P("dp", "section", None, None),
        ),
        out_specs=(P("section", None, "dp"), P("dp", "section", None, None)),
        check_vma=False,
    )
```

```python
import functools

import jax
import jax.numpy as jnp
from jax import lax
from jax.experimental import pallas as pl
from jax.experimental.pallas import tpu as pltpu
from jax.sharding import PartitionSpec as P

norm_eps = 1e-06
learn_rate = 1.0
MESH = pl.DeviceIdType.MESH
SPLIT = 2


def flipped(me, mask):
    out, bit, left = me, 1, mask
    while left:
        if left & 1:
            out = out + bit * (1 - 2 * ((me // bit) % 2))
        left >>= 1
        bit <<= 1
    return out


def spans(order):
    masks = [0]
    for bit in order:
        masks = masks + [mask ^ bit for mask in masks]
    return masks


def relay(n_rep, sections, chunk, rate, x_hbm, cot_hbm, w_hbm, g_hbm, now_hbm,
          u_hbm, q_hbm, base_hbm, far_hbm,
          u_ref, q_ref, wf, weight, turned, xin, dyin, ybuf, dxbuf, zbuf, rbuf, dubuf, local, part_sum, landed,
          tok, zout, zland, load_sem, x_sem, cot_sem, local_sem,
          ag_send, ag_recv, rs_send, rs_recv, f_send, f_recv, b_send, b_recv,
          z_send, z_recv, now_sem, base_sem, act_sem, gate, back):
    me = lax.axis_index("dp")
    sec = lax.axis_index("section")
    last = sections - 1
    rows, width = x_hbm.shape
    cols = width // n_rep
    half = width // 2
    n_chunks = rows // chunk
    inv = width ** (-0.5)
    bits = [1 << i for i in range(n_rep.bit_length() - 1)]
    orders = (bits, bits[::-1])

    for part in range(2):
        sl = pl.ds(part * half, half)
        copy = pltpu.make_async_copy(w_hbm.at[sl, :], wf.at[sl, :], load_sem.at[part])
        copy.start()

    def x_load(j):
        return pltpu.make_async_copy(
            x_hbm.at[:, pl.ds(j * cols, cols)], xin.at[j], x_sem.at[j])

    def cot_load(j):
        return pltpu.make_async_copy(
            cot_hbm.at[:, pl.ds(j * cols, cols)], dyin.at[j], cot_sem.at[j])

    @pl.when(sec == 0)
    def _():
        for j in range(n_rep):
            x_load(j).start()

    @pl.when(sec == last)
    def _():
        for j in range(n_rep):
            cot_load(j).start()

    def g_block(part, mask):
        at = pl.multiple_of(flipped(me, mask) * cols, cols)
        return g_hbm.at[pl.ds(part * half, half), pl.ds(at, cols)]

    barrier = pltpu.get_barrier_semaphore()
    for mask in range(1, n_rep):
        pl.semaphore_signal(barrier, inc=1, device_id={"dp": flipped(me, mask)}, device_id_type=MESH)

    @pl.when(sec > 0)
    def _():
        pl.semaphore_signal(barrier, inc=1, device_id={"section": sec - 1}, device_id_type=MESH)

    @pl.when(sec < last)
    def _():
        pl.semaphore_signal(barrier, inc=1, device_id={"section": sec + 1}, device_id_type=MESH)

    neighbours = (sec + last) // sections + (2 * last - sec) // sections
    pl.semaphore_wait(barrier, n_rep - 1 + neighbours)

    def piece_of(tokens, part, mask):
        if tokens:
            return tok.at[flipped(me, mask), pl.ds(part * (rows // 2), rows // 2), :]
        return weight.at[flipped(me, mask), pl.ds(part * half, half), :]

    def ag_copy(tokens, part, mask, bit):
        ref = piece_of(tokens, part, mask)
        return pltpu.make_async_remote_copy(
            src_ref=ref, dst_ref=ref,
            send_sem=ag_send.at[part, mask ^ bit], recv_sem=ag_recv.at[part, mask ^ bit],
            device_id={"dp": flipped(me, bit)}, device_id_type=MESH)

    def ag_arrival(tokens, part, mask):
        ref = piece_of(tokens, part, mask)
        return pltpu.make_async_remote_copy(
            src_ref=ref, dst_ref=ref,
            send_sem=ag_send.at[part, mask], recv_sem=ag_recv.at[part, mask],
            device_id={"dp": flipped(me, mask)}, device_id_type=MESH)

    def gather(tokens, prepare):
        for part in range(2):
            prepare(part)
            ag_copy(tokens, part, 0, orders[part][0]).start()
        for step in range(1, len(bits)):
            for part in range(2):
                ag_copy(tokens, part, 0, orders[part][step]).start()
        arrived = set()
        for step in range(1, len(bits)):
            for index in range(1, 1 << step):
                for part in range(2):
                    this = spans(orders[part][:step])[index]
                    if (part, this) not in arrived:
                        ag_arrival(tokens, part, this).wait_recv()
                        arrived.add((part, this))
                    ag_copy(tokens, part, this, orders[part][step]).start()
        return arrived

    def gather_sent(tokens, masks):
        for part in range(2):
            for mask in masks:
                ag_copy(tokens, part, 0, mask).wait_send()

    everyone = range(1, n_rep)
    relayed = [mask for mask in everyone if mask not in bits]

    def cast(part):
        pltpu.make_async_copy(
            w_hbm.at[pl.ds(part * half, half), :], wf.at[pl.ds(part * half, half), :],
            load_sem.at[part]).wait()
        piece = half // 4
        for i in range(4):
            sl = pl.ds(part * half + i * piece, piece)
            weight[me, sl, :] = wf[sl, :].astype(jnp.bfloat16)

    def normalise(sl):
        square = jnp.zeros((chunk, 1), jnp.float32)
        for j in range(n_rep):
            x = xin[j, sl, :].astype(jnp.float32)
            square += jnp.sum(x * x, axis=-1, keepdims=True)
        scale = lax.rsqrt(square * (1.0 / width) + norm_eps)
        rbuf[sl, :] = scale
        for j in range(n_rep):
            x = xin[j, sl, :].astype(jnp.float32)
            u_ref[sl, pl.ds(j * cols, cols)] = (x * scale).astype(jnp.bfloat16)

    def z_copy(part, mask):
        sl = pl.ds(part * (rows // 2), rows // 2)
        return pltpu.make_async_remote_copy(
            src_ref=zout.at[mask, sl, :], dst_ref=zland.at[me, sl, :],
            send_sem=z_send.at[part, mask], recv_sem=z_recv.at[part, mask],
            device_id={"dp": flipped(me, mask)}, device_id_type=MESH)

    def z_arrival(part, mask):
        sl = pl.ds(part * (rows // 2), rows // 2)
        return pltpu.make_async_remote_copy(
            src_ref=zout.at[mask, sl, :], dst_ref=zland.at[flipped(me, mask), sl, :],
            send_sem=z_send.at[part, mask], recv_sem=z_recv.at[part, mask],
            device_id={"dp": flipped(me, mask)}, device_id_type=MESH)

    odd = lax.rem(sec, 2) == 1

    def turn():
        @pl.loop(0, n_rep)
        def _(j):
            for k in range(n_rep):
                span = pl.ds(k * cols, cols)
                turned[j, :, span] = weight[j, span, :].T

    @pl.when(sec == 0)
    def _():
        for j in range(n_rep):
            x_load(j).wait()

        def prepare(part):
            @pl.loop(part * (n_chunks // 2), (part + 1) * (n_chunks // 2))
            def _(c):
                sl = pl.ds(pl.multiple_of(c * chunk, chunk), chunk)
                normalise(sl)
                tok[me, sl, :] = u_ref[sl, :]

        arrived = gather(True, prepare)
        for part in range(2):
            cast(part)
        for mask in range(n_rep):
            for part in range(2):
                if mask and (part, mask) not in arrived:
                    ag_arrival(True, part, mask).wait_recv()
                sl = pl.ds(part * (rows // 2), rows // 2)
                z = jnp.dot(tok[flipped(me, mask), sl, :], weight[me],
                            preferred_element_type=jnp.float32) * inv
                if mask:
                    zout[mask, sl, :] = z.astype(jnp.bfloat16)
                    z_copy(part, mask).start()
                else:
                    zbuf[me, sl, :] = z
        gather_sent(True, everyone)

    @pl.when((sec > 0) & jnp.logical_not(odd))
    def _():
        arrived = gather(False, cast)
        gather_sent(False, bits)
        pl.semaphore_signal(
            gate, inc=1, device_id={"section": jnp.minimum(sec + 1, last)}, device_id_type=MESH)
        gather_sent(False, relayed)
        for part in range(2):
            for mask in range(1, n_rep):
                if (part, mask) not in arrived:
                    ag_arrival(False, part, mask).wait_recv()
        turn()

    def rs_send_copy(part, step, mask, source):
        bit = orders[part][step]
        slot = mask ^ bit
        if step == len(bits) - 1:
            target = far_hbm.at[pl.ds(part * half, half), :]
        else:
            target = landed.at[part, slot_of(part, step, slot)]
        return pltpu.make_async_remote_copy(
            src_ref=source, dst_ref=target,
            send_sem=rs_send.at[part, slot_of(part, step, slot)],
            recv_sem=rs_recv.at[part, slot_of(part, step, slot)],
            device_id={"dp": flipped(me, bit)}, device_id_type=MESH)

    def kept(part, step):
        return sorted(spans(orders[part][step:]))

    def ordered(part, step):
        return sorted(kept(part, step), key=lambda mask: (not mask & orders[part][step], mask))

    def slot_of(part, step, mask):
        base = sum(len(kept(part, s + 1)) for s in range(step))
        return base + kept(part, step + 1).index(mask)

    def local_copy(part, mask):
        at = kept(part, 1).index(mask)
        return pltpu.make_async_copy(
            g_block(part, mask), local.at[part, at], local_sem.at[part, at])

    def rs_start():
        for mask_at in range(n_rep // 2):
            for part in range(2):
                mask = ordered(part, 1)[mask_at] ^ orders[part][0]
                rs_send_copy(part, 0, mask, g_block(part, mask)).start()
        for part in range(2):
            for mask in ordered(part, 1):
                local_copy(part, mask).start()

    early = sections // 2

    @pl.when(odd)
    def _():
        @pl.when(sec > 1)
        def _():
            pl.semaphore_wait(gate, 1)

        arrived = gather(False, cast)
        gather_sent(False, everyone)
        pl.semaphore_signal(
            back, inc=1, device_id={"section": jnp.maximum(sec - 1, 0)}, device_id_type=MESH)
        rs_start()
        for part in range(2):
            for mask in range(1, n_rep):
                if (part, mask) not in arrived:
                    ag_arrival(False, part, mask).wait_recv()

    @pl.when(odd & (sec >= early))
    def _():
        turn()

    @pl.when(jnp.logical_not(odd) & (sec >= early))
    def _():
        pl.semaphore_wait(back, 1)
        rs_start()

    def now_load(part):
        sl = pl.ds(part * half, half)
        return pltpu.make_async_copy(now_hbm.at[sl, :], wf.at[sl, :], now_sem.at[part])

    def base_store(part):
        sl = pl.ds(part * half, half)
        return pltpu.make_async_copy(wf.at[sl, :], base_hbm.at[sl, :], base_sem.at[part])

    def act_store(c, i):
        sl = pl.ds(pl.multiple_of(c * chunk, chunk), chunk)
        source, target = ((u_ref, u_hbm), (q_ref, q_hbm))[i]
        return pltpu.make_async_copy(source.at[sl, :], target.at[sl, :], act_sem.at[i, c])

    for part in range(2):
        now_load(part).start()

    def f_copy(c, j):
        sl = pl.ds(pl.multiple_of(c * chunk, chunk), chunk)
        return pltpu.make_async_remote_copy(
            src_ref=ybuf.at[j, sl, :], dst_ref=xin.at[j, sl, :],
            send_sem=f_send.at[c, j], recv_sem=f_recv.at[c, j],
            device_id={"section": jnp.minimum(sec + 1, last)}, device_id_type=MESH)

    def b_copy(c, j):
        sl = pl.ds(pl.multiple_of(c * chunk, chunk), chunk)
        return pltpu.make_async_remote_copy(
            src_ref=dxbuf.at[j, sl, :], dst_ref=dyin.at[j, sl, :],
            send_sem=b_send.at[c, j], recv_sem=b_recv.at[c, j],
            device_id={"section": jnp.maximum(sec - 1, 0)}, device_id_type=MESH)

    @pl.when(sec == 0)
    def _():
        for part in range(2):
            for mask in range(1, n_rep):
                z_arrival(part, mask).wait_recv()
                sl = pl.ds(part * (rows // 2), rows // 2)
                zbuf[flipped(me, mask), sl, :] = zland[flipped(me, mask), sl, :].astype(jnp.float32)

    @pl.when(sec == last)
    def _():
        for j in range(n_rep):
            cot_load(j).wait()

    def section_input(c):
        for j in range(n_rep):
            f_copy(c, j).wait_recv()
        normalise(pl.ds(pl.multiple_of(c * chunk, chunk), chunk))

    def project(c, j):
        sl = pl.ds(pl.multiple_of(c * chunk, chunk), chunk)
        zbuf[j, sl, :] = jnp.dot(
            u_ref[sl, :], weight[j], preferred_element_type=jnp.float32) * inv

    def emit(c, j):
        sl = pl.ds(pl.multiple_of(c * chunk, chunk), chunk)
        zz = zbuf[j, sl, :]
        y = xin[j, sl, :].astype(jnp.float32) + zz * jax.nn.sigmoid(zz)
        ybuf[j, sl, :] = y.astype(jnp.bfloat16)
        f_copy(c, j).start()

    def small_grad(c, j):
        sl = pl.ds(pl.multiple_of(c * chunk, chunk), chunk)
        z = zbuf[j, sl, :]
        sig = jax.nn.sigmoid(z)
        dz = dyin[j, sl, :].astype(jnp.float32) * sig * (1.0 + z * (1.0 - sig))
        q_ref[sl, pl.ds(j * cols, cols)] = (dz * inv).astype(jnp.bfloat16)

    def back_project(c, j):
        sl = pl.ds(pl.multiple_of(c * chunk, chunk), chunk)
        q = q_ref[sl, pl.ds(j * cols, cols)]
        for k in range(n_rep):
            du = jnp.dot(q, turned[j, :, pl.ds(k * cols, cols)], preferred_element_type=jnp.float32)
            dubuf[k] = du if j == 0 else dubuf[k] + du

    def emit_back(c):
        sl = pl.ds(pl.multiple_of(c * chunk, chunk), chunk)
        scale = rbuf[sl, :]
        dot_sum = jnp.zeros((chunk, 1), jnp.float32)
        for k in range(n_rep):
            normed = xin[k, sl, :].astype(jnp.float32) * scale
            dot_sum += jnp.sum(dubuf[k] * normed, axis=-1, keepdims=True)
        mean = dot_sum * (1.0 / width)
        for k in range(n_rep):
            normed = xin[k, sl, :].astype(jnp.float32) * scale
            dx = dyin[k, sl, :].astype(jnp.float32) + scale * (dubuf[k] - normed * mean)
            dxbuf[k, sl, :] = dx.astype(jnp.bfloat16)
            b_copy(c, k).start()
        for i in range(2):
            act_store(c, i).start()

    middle = (sec > 0) & (sec < last)

    @pl.when(sec == 0)
    def _():
        @pl.loop(0, n_chunks)
        def _(c):
            for j in range(n_rep):
                emit(c, j)

    @pl.when(middle)
    def _():
        @pl.loop(0, n_chunks)
        def _(c):
            section_input(c)
            for j in range(n_rep):
                project(c, j)
                emit(c, j)

    def rs_add(step, part, mask):
        rs_send_copy(part, step - 1, mask ^ orders[part][step - 1],
                     landed.at[part, 0]).wait_recv()
        at = kept(part, 1).index(mask)
        if step == 1:
            local_copy(part, mask).wait()
        if step == 1 and not mask:
            now_load(part).wait()
        pieces = 4
        piece = half // pieces
        for i in range(pieces):
            ps = pl.ds(i * piece, piece)
            total = landed[part, slot_of(part, step - 1, mask), ps, :].astype(jnp.float32)
            if step == 1:
                total = local[part, at, ps, :].astype(jnp.float32) + total
            elif mask:
                total = part_sum[part, at, ps, :].astype(jnp.float32) + total
            if mask:
                part_sum[part, at, ps, :] = total.astype(jnp.bfloat16)
            else:
                held = pl.ds(part * half + i * piece, piece)
                wf[held, :] = wf[held, :] - rate * total
        if not mask and step == len(bits) - 1:
            base_store(part).start()
        if mask & orders[part][step]:
            rs_send_copy(part, step, mask, part_sum.at[part, at]).start()

    def rs_middle(first):
        for step in range(1, len(bits)):
            for index in range(len(kept(0, step))):
                for part in range(2):
                    mask = ordered(part, step)[index]
                    if first == (step == 1 and mask & orders[part][1] > 0):
                        rs_add(step, part, mask)

    @pl.when(odd & (sec < early))
    def _():
        turn()

    @pl.when(jnp.logical_not(odd) & (sec < early))
    def _():
        pl.semaphore_wait(back, 1)
        rs_start()

    @pl.when(sec < early)
    def _():
        rs_middle(True)

    @pl.when(sec < 2)
    def _():
        rs_middle(False)

    @pl.when(sec == 0)
    def _():
        @pl.loop(0, n_chunks)
        def _(c):
            for j in range(n_rep):
                b_copy(c, j).wait_recv()
                small_grad(c, j)
            for i in range(2):
                act_store(c, i).start()

    @pl.when(middle)
    def _():
        @pl.loop(0, n_chunks)
        def _(c):
            for j in range(n_rep):
                b_copy(c, j).wait_recv()
                small_grad(c, j)
                back_project(c, j)
            emit_back(c)

    @pl.when(sec == last)
    def _():
        @pl.loop(0, n_chunks)
        def _(c):
            section_input(c)
            for j in range(n_rep):
                project(c, j)
            for j in range(n_rep):
                small_grad(c, j)
                back_project(c, j)
            emit_back(c)

    @pl.when(sec >= early)
    def _():
        rs_middle(True)

    @pl.when(sec >= 2)
    def _():
        rs_middle(False)

    final = len(bits) - 1
    for part in range(2):
        rs_send_copy(part, final, orders[part][final], part_sum.at[part, 0]).wait_recv()
    @pl.when(sec == 0)
    def _():
        for part in range(2):
            for mask in range(1, n_rep):
                z_copy(part, mask).wait_send()

    for part in range(2):
        for step in range(len(bits)):
            for mask in kept(part, step + 1):
                rs_send_copy(part, step, mask ^ orders[part][step], part_sum.at[part, 0]).wait_send()

    for part in range(2):
        base_store(part).wait()

    @pl.loop(0, n_chunks)
    def _(c):
        for i in range(2):
            act_store(c, i).wait()

    @pl.when(sec < last)
    def _():
        @pl.loop(0, n_chunks)
        def _(c):
            for j in range(n_rep):
                f_copy(c, j).wait_send()

    @pl.when(sec > 0)
    def _():
        @pl.loop(0, n_chunks)
        def _(c):
            for j in range(n_rep):
                b_copy(c, j).wait_send()


def finish(rate, u_hbm, q_hbm, base_hbm, far_hbm, next_hbm, grad_hbm,
           u_ref, q_ref, base_ref, far_ref, next_ref, grad_ref, act_sem, in_sem, next_sem, grad_sem):
    tile = next_ref.shape[1]
    count = next_ref.shape[0]

    def act_load(i):
        source, target = ((u_hbm, u_ref), (q_hbm, q_ref))[i]
        return pltpu.make_async_copy(source, target, act_sem.at[i])

    def loads(t):
        rows = pl.ds(t * tile, tile)
        pairs = ((base_hbm, base_ref), (far_hbm, far_ref))
        return [pltpu.make_async_copy(source.at[rows, :], target.at[t], in_sem.at[i, t])
                for i, (source, target) in enumerate(pairs)]

    def next_store(t):
        return pltpu.make_async_copy(
            next_ref.at[t], next_hbm.at[pl.ds(t * tile, tile), :], next_sem.at[t])

    def grad_store(t):
        return pltpu.make_async_copy(
            grad_ref.at[t], grad_hbm.at[pl.ds(t * tile, tile), :], grad_sem.at[t])

    for i in range(2):
        act_load(i).start()
    for t in range(count):
        for copy in loads(t):
            copy.start()
    for i in range(2):
        act_load(i).wait()
    for t in range(count):
        grad_ref[t] = lax.dot_general(
            u_ref[:, pl.ds(t * tile, tile)], q_ref[...], (((0,), (0,)), ((), ())),
            preferred_element_type=jnp.float32).astype(jnp.bfloat16)
        grad_store(t).start()
        for copy in loads(t):
            copy.wait()
        next_ref[t] = base_ref[t] - rate * far_ref[t].astype(jnp.float32)
        next_store(t).start()
    for t in range(count):
        grad_store(t).wait()
        next_store(t).wait()


def body(inputs, cotangent, w_prev, w_now, grads_prev):
    sections = lax.axis_size("section")
    n_rep = lax.axis_size("dp")
    micro, tok_mb, width = inputs.shape
    rows = micro * tok_mb
    cols = width // n_rep
    half = width // 2
    chunk = tok_mb // SPLIT
    n_chunks = rows // chunk
    any_spec = pl.BlockSpec(memory_space=pl.ANY)
    bf16, f32 = jnp.bfloat16, jnp.float32
    dma = pltpu.SemaphoreType.DMA
    rate = learn_rate / n_rep
    upper, small, base, far = pl.pallas_call(
        functools.partial(relay, n_rep, sections, chunk, rate),
        out_shape=(
            jax.ShapeDtypeStruct((rows, width), bf16),
            jax.ShapeDtypeStruct((rows, width), bf16),
            jax.ShapeDtypeStruct((width, cols), f32),
            jax.ShapeDtypeStruct((width, cols), bf16),
        ),
        in_specs=[any_spec] * 5,
        out_specs=(any_spec,) * 4,
        scratch_shapes=[
            pltpu.VMEM((rows, width), bf16),
            pltpu.VMEM((rows, width), bf16),
            pltpu.VMEM((width, cols), f32),
            pltpu.VMEM((n_rep, width, cols), bf16),
            pltpu.VMEM((n_rep, cols, width), bf16),
            pltpu.VMEM((n_rep, rows, cols), bf16),
            pltpu.VMEM((n_rep, rows, cols), bf16),
            pltpu.VMEM((n_rep, rows, cols), bf16),
            pltpu.VMEM((n_rep, rows, cols), bf16),
            pltpu.VMEM((n_rep, rows, cols), f32),
            pltpu.VMEM((rows, 1), f32),
            pltpu.VMEM((n_rep, chunk, cols), f32),
            pltpu.VMEM((2, n_rep // 2, half, cols), bf16),
            pltpu.VMEM((2, n_rep // 2, half, cols), bf16),
            pltpu.VMEM((2, max(1, n_rep - 2), half, cols), bf16),
            pltpu.VMEM((n_rep, rows, width), bf16),
            pltpu.VMEM((n_rep, rows, cols), bf16),
            pltpu.VMEM((n_rep, rows, cols), bf16),
            dma((2,)), dma((n_rep,)), dma((n_rep,)), dma((2, n_rep // 2)),
            dma((2, n_rep)), dma((2, n_rep)),
            dma((2, n_rep)), dma((2, n_rep)),
            dma((n_chunks, n_rep)), dma((n_chunks, n_rep)),
            dma((n_chunks, n_rep)), dma((n_chunks, n_rep)),
            dma((2, n_rep)), dma((2, n_rep)),
            dma((2,)), dma((2,)), dma((2, n_chunks)),
            pltpu.SemaphoreType.REGULAR, pltpu.SemaphoreType.REGULAR,
        ],
        compiler_params=pltpu.CompilerParams(
            collective_id=0, has_side_effects=True, vmem_limit_bytes=60 * 1024 * 1024
        ),
        name="relay",
    )(inputs.reshape(rows, width), cotangent.reshape(rows, width), w_prev[0], grads_prev[0, 0], w_now[0])
    count = 8
    tile = width // count
    w_next, grads_next = pl.pallas_call(
        functools.partial(finish, rate),
        out_shape=(
            jax.ShapeDtypeStruct((width, cols), f32),
            jax.ShapeDtypeStruct((width, width), bf16),
        ),
        in_specs=[any_spec] * 4,
        out_specs=(any_spec,) * 2,
        scratch_shapes=[
            pltpu.VMEM((rows, width), bf16),
            pltpu.VMEM((rows, width), bf16),
            pltpu.VMEM((count, tile, cols), f32),
            pltpu.VMEM((count, tile, cols), bf16),
            pltpu.VMEM((count, tile, cols), f32),
            pltpu.VMEM((count, tile, width), bf16),
            dma((2,)), dma((2, count)), dma((count,)), dma((count,)),
        ],
        compiler_params=pltpu.CompilerParams(vmem_limit_bytes=60 * 1024 * 1024),
        name="finish",
    )(upper, small, base, far)
    return (w_next[None], grads_next[None, None])


def solution(mesh):
    return jax.shard_map(
        body,
        mesh=mesh,
        in_specs=(
            P(None, "dp", None),
            P(None, "dp", None),
            P("section", None, "dp"),
            P("section", None, "dp"),
            P("dp", "section", None, None),
        ),
        out_specs=(P("section", None, "dp"), P("dp", "section", None, None)),
        check_vma=False,
    )
```

```python
import functools

import jax
import jax.numpy as jnp
from jax import lax
from jax.experimental import pallas as pl
from jax.experimental.pallas import tpu as pltpu
from jax.sharding import PartitionSpec as P

norm_eps = 1e-06
learn_rate = 1.0
MESH = pl.DeviceIdType.MESH
SPLIT = 2


def flipped(me, mask):
    out, bit, left = me, 1, mask
    while left:
        if left & 1:
            out = out + bit * (1 - 2 * ((me // bit) % 2))
        left >>= 1
        bit <<= 1
    return out


def spans(order):
    masks = [0]
    for bit in order:
        masks = masks + [mask ^ bit for mask in masks]
    return masks


def relay(n_rep, sections, chunk, rate, x_hbm, cot_hbm, w_hbm, g_hbm, now_hbm,
          u_hbm, q_hbm, base_hbm, far_hbm,
          u_ref, q_ref, wf, weight, turned, xin, dyin, ybuf, dxbuf, zbuf, rbuf, dubuf, local, landed,
          load_sem, x_sem, cot_sem, local_sem,
          ag_send, ag_recv, rs_send, rs_recv, f_send, f_recv, b_send, b_recv,
          z_send, z_recv, now_sem, base_sem, act_sem, gate, back):
    me = lax.axis_index("dp")
    sec = lax.axis_index("section")
    last = sections - 1
    rows, width = x_hbm.shape
    cols = width // n_rep
    half = width // 2
    n_chunks = rows // chunk
    inv = width ** (-0.5)
    fill = half // 4
    bits = [1 << i for i in range(n_rep.bit_length() - 1)]
    orders = (bits, bits[::-1])

    for part in range(2):
        sl = pl.ds(part * half, half)
        copy = pltpu.make_async_copy(w_hbm.at[sl, :], wf.at[sl, :], load_sem.at[part])
        copy.start()

    def x_load(j):
        return pltpu.make_async_copy(
            x_hbm.at[:, pl.ds(j * cols, cols)], xin.at[j], x_sem.at[j])

    def cot_load(j):
        return pltpu.make_async_copy(
            cot_hbm.at[:, pl.ds(j * cols, cols)], dyin.at[j], cot_sem.at[j])

    @pl.when(sec == 0)
    def _():
        for j in range(n_rep):
            x_load(j).start()

    @pl.when(sec == last)
    def _():
        for j in range(n_rep):
            cot_load(j).start()

    def g_block(part, mask):
        at = pl.multiple_of(flipped(me, mask) * cols, cols)
        return g_hbm.at[pl.ds(part * half, half), pl.ds(at, cols)]

    barrier = pltpu.get_barrier_semaphore()
    for mask in range(1, n_rep):
        pl.semaphore_signal(barrier, inc=1, device_id={"dp": flipped(me, mask)}, device_id_type=MESH)

    @pl.when(sec > 0)
    def _():
        pl.semaphore_signal(barrier, inc=1, device_id={"section": sec - 1}, device_id_type=MESH)

    @pl.when(sec < last)
    def _():
        pl.semaphore_signal(barrier, inc=1, device_id={"section": sec + 1}, device_id_type=MESH)

    neighbours = (sec + last) // sections + (2 * last - sec) // sections
    pl.semaphore_wait(barrier, n_rep - 1 + neighbours)

    def piece_of(tokens, part, mask):
        if tokens:
            return turned.at[flipped(me, mask), pl.ds(part * (rows // 2), rows // 2), :]
        return weight.at[flipped(me, mask), pl.ds(part * half, half), :]

    def ag_copy(tokens, part, mask, bit):
        ref = piece_of(tokens, part, mask)
        return pltpu.make_async_remote_copy(
            src_ref=ref, dst_ref=ref,
            send_sem=ag_send.at[part, mask ^ bit], recv_sem=ag_recv.at[part, mask ^ bit],
            device_id={"dp": flipped(me, bit)}, device_id_type=MESH)

    def ag_arrival(tokens, part, mask):
        ref = piece_of(tokens, part, mask)
        return pltpu.make_async_remote_copy(
            src_ref=ref, dst_ref=ref,
            send_sem=ag_send.at[part, mask], recv_sem=ag_recv.at[part, mask],
            device_id={"dp": flipped(me, mask)}, device_id_type=MESH)

    def gather(tokens, prepare):
        for part in range(2):
            prepare(part)
            ag_copy(tokens, part, 0, orders[part][0]).start()
        for step in range(1, len(bits)):
            for part in range(2):
                ag_copy(tokens, part, 0, orders[part][step]).start()
        arrived = set()
        for step in range(1, len(bits)):
            for index in range(1, 1 << step):
                for part in range(2):
                    this = spans(orders[part][:step])[index]
                    if (part, this) not in arrived:
                        ag_arrival(tokens, part, this).wait_recv()
                        arrived.add((part, this))
                    ag_copy(tokens, part, this, orders[part][step]).start()
        return arrived

    def gather_sent(tokens, masks):
        for part in range(2):
            for mask in masks:
                ag_copy(tokens, part, 0, mask).wait_send()

    everyone = range(1, n_rep)
    relayed = [mask for mask in everyone if mask not in bits]

    def cast(part):
        pltpu.make_async_copy(
            w_hbm.at[pl.ds(part * half, half), :], wf.at[pl.ds(part * half, half), :],
            load_sem.at[part]).wait()
        piece = half // 4
        for i in range(4):
            sl = pl.ds(part * half + i * piece, piece)
            weight[me, sl, :] = wf[sl, :].astype(jnp.bfloat16)

    def normalise(sl):
        square = jnp.zeros((chunk, 1), jnp.float32)
        for j in range(n_rep):
            x = xin[j, sl, :].astype(jnp.float32)
            square += jnp.sum(x * x, axis=-1, keepdims=True)
        scale = lax.rsqrt(square * (1.0 / width) + norm_eps)
        rbuf[sl, :] = scale
        for j in range(n_rep):
            x = xin[j, sl, :].astype(jnp.float32)
            u_ref[sl, pl.ds(j * cols, cols)] = (x * scale).astype(jnp.bfloat16)

    def z_copy(part, mask):
        sl = pl.ds(part * (rows // 2), rows // 2)
        return pltpu.make_async_remote_copy(
            src_ref=dxbuf.at[mask, sl, :], dst_ref=dyin.at[me, sl, :],
            send_sem=z_send.at[part, mask], recv_sem=z_recv.at[part, mask],
            device_id={"dp": flipped(me, mask)}, device_id_type=MESH)

    def z_arrival(part, mask):
        sl = pl.ds(part * (rows // 2), rows // 2)
        return pltpu.make_async_remote_copy(
            src_ref=dxbuf.at[mask, sl, :], dst_ref=dyin.at[flipped(me, mask), sl, :],
            send_sem=z_send.at[part, mask], recv_sem=z_recv.at[part, mask],
            device_id={"dp": flipped(me, mask)}, device_id_type=MESH)

    odd = lax.rem(sec, 2) == 1

    def rs_send_copy(part, step, mask, source):
        bit = orders[part][step]
        slot = mask ^ bit
        if step == len(bits) - 1:
            target = far_hbm.at[pl.ds(part * half, half), :]
        else:
            target = landed.at[part, slot_of(part, step, slot)]
        return pltpu.make_async_remote_copy(
            src_ref=source, dst_ref=target,
            send_sem=rs_send.at[part, slot_of(part, step, slot)],
            recv_sem=rs_recv.at[part, slot_of(part, step, slot)],
            device_id={"dp": flipped(me, bit)}, device_id_type=MESH)

    def kept(part, step):
        return sorted(spans(orders[part][step:]))

    def ordered(part, step):
        return sorted(kept(part, step), key=lambda mask: (not mask & orders[part][step], mask))

    def slot_of(part, step, mask):
        base = sum(len(kept(part, s + 1)) for s in range(step))
        return base + kept(part, step + 1).index(mask)

    def local_copy(part, mask):
        at = kept(part, 1).index(mask)
        return pltpu.make_async_copy(
            g_block(part, mask), local.at[part, at], local_sem.at[part, at])

    def rs_rows(part, mask, low, high):
        span = pl.ds(low, high - low)
        slot = slot_of(part, 0, mask ^ orders[part][0])
        pltpu.make_async_remote_copy(
            src_ref=g_block(part, mask).at[span, :], dst_ref=landed.at[part, slot, span, :],
            send_sem=rs_send.at[part, slot], recv_sem=rs_recv.at[part, slot],
            device_id={"dp": flipped(me, orders[part][0])}, device_id_type=MESH).start()

    def rs_early():
        for part in range(2):
            rs_rows(part, ordered(part, 1)[-1] ^ orders[part][0], 0, fill)

    def rs_start(done):
        for mask_at in range(n_rep // 2):
            for part in range(2):
                mask = ordered(part, 1)[mask_at] ^ orders[part][0]
                rs_rows(part, mask, done if mask_at == n_rep // 2 - 1 else 0, half)
        for part in range(2):
            for mask in ordered(part, 1):
                local_copy(part, mask).start()

    @pl.when(odd & (sec > 1))
    def _():
        rs_early()

    def turn():
        @pl.loop(0, n_rep)
        def _(j):
            for k in range(n_rep):
                span = pl.ds(k * cols, cols)
                turned[j, pl.ds(0, cols), span] = weight[j, span, :].T

    @pl.when(sec == 0)
    def _():
        for j in range(n_rep):
            x_load(j).wait()

        def prepare(part):
            @pl.loop(part * (n_chunks // 2), (part + 1) * (n_chunks // 2))
            def _(c):
                sl = pl.ds(pl.multiple_of(c * chunk, chunk), chunk)
                normalise(sl)
                turned[me, sl, :] = u_ref[sl, :]

        arrived = gather(True, prepare)
        for part in range(2):
            cast(part)
        for mask in range(n_rep):
            for part in range(2):
                if mask and (part, mask) not in arrived:
                    ag_arrival(True, part, mask).wait_recv()
                sl = pl.ds(part * (rows // 2), rows // 2)
                z = jnp.dot(turned[flipped(me, mask), sl, :], weight[me],
                            preferred_element_type=jnp.float32) * inv
                if mask:
                    dxbuf[mask, sl, :] = z.astype(jnp.bfloat16)
                    z_copy(part, mask).start()
                else:
                    zbuf[me, sl, :] = z
        gather_sent(True, everyone)

    @pl.when((sec > 0) & jnp.logical_not(odd))
    def _():
        arrived = gather(False, cast)
        gather_sent(False, bits)
        pl.semaphore_signal(
            gate, inc=1, device_id={"section": jnp.minimum(sec + 1, last)}, device_id_type=MESH)
        gather_sent(False, relayed)
        for part in range(2):
            for mask in range(1, n_rep):
                if (part, mask) not in arrived:
                    ag_arrival(False, part, mask).wait_recv()
        turn()

    early = sections // 2

    @pl.when(odd)
    def _():
        @pl.when(sec > 1)
        def _():
            pl.semaphore_wait(gate, 1)

        arrived = gather(False, cast)

        @pl.when(sec >= 2)
        def _():
            rs_start(fill)

        gather_sent(False, everyone)
        pl.semaphore_signal(
            back, inc=1, device_id={"section": jnp.maximum(sec - 1, 0)}, device_id_type=MESH)

        @pl.when(sec == 1)
        def _():
            rs_early()

        @pl.when(sec < 2)
        def _():
            rs_start(fill)

        for part in range(2):
            for mask in range(1, n_rep):
                if (part, mask) not in arrived:
                    ag_arrival(False, part, mask).wait_recv()

    @pl.when(odd & (sec >= early))
    def _():
        turn()

    @pl.when(jnp.logical_not(odd) & (sec >= early))
    def _():
        pl.semaphore_wait(back, 1)
        rs_start(0)

    def now_load(part):
        sl = pl.ds(part * half, half)
        return pltpu.make_async_copy(now_hbm.at[sl, :], wf.at[sl, :], now_sem.at[part])

    def base_store(part):
        sl = pl.ds(part * half, half)
        return pltpu.make_async_copy(wf.at[sl, :], base_hbm.at[sl, :], base_sem.at[part])

    def act_store(c, i):
        sl = pl.ds(pl.multiple_of(c * chunk, chunk), chunk)
        source, target = ((u_ref, u_hbm), (q_ref, q_hbm))[i]
        return pltpu.make_async_copy(source.at[sl, :], target.at[sl, :], act_sem.at[i, c])

    for part in range(2):
        now_load(part).start()

    def f_copy(c, j):
        sl = pl.ds(pl.multiple_of(c * chunk, chunk), chunk)
        return pltpu.make_async_remote_copy(
            src_ref=ybuf.at[j, sl, :], dst_ref=xin.at[j, sl, :],
            send_sem=f_send.at[c, j], recv_sem=f_recv.at[c, j],
            device_id={"section": jnp.minimum(sec + 1, last)}, device_id_type=MESH)

    def b_copy(c, j):
        sl = pl.ds(pl.multiple_of(c * chunk, chunk), chunk)
        return pltpu.make_async_remote_copy(
            src_ref=dxbuf.at[j, sl, :], dst_ref=dyin.at[j, sl, :],
            send_sem=b_send.at[c, j], recv_sem=b_recv.at[c, j],
            device_id={"section": jnp.maximum(sec - 1, 0)}, device_id_type=MESH)

    @pl.when(sec == 0)
    def _():
        for part in range(2):
            for mask in range(1, n_rep):
                z_arrival(part, mask).wait_recv()
                sl = pl.ds(part * (rows // 2), rows // 2)
                zbuf[flipped(me, mask), sl, :] = dyin[flipped(me, mask), sl, :].astype(jnp.float32)

    @pl.when(sec == last)
    def _():
        for j in range(n_rep):
            cot_load(j).wait()

    def section_input(c):
        for j in range(n_rep):
            f_copy(c, j).wait_recv()
        normalise(pl.ds(pl.multiple_of(c * chunk, chunk), chunk))

    def project(c, j):
        sl = pl.ds(pl.multiple_of(c * chunk, chunk), chunk)
        zbuf[j, sl, :] = jnp.dot(
            u_ref[sl, :], weight[j], preferred_element_type=jnp.float32) * inv

    def emit(c, j):
        sl = pl.ds(pl.multiple_of(c * chunk, chunk), chunk)
        zz = zbuf[j, sl, :]
        y = xin[j, sl, :].astype(jnp.float32) + zz * jax.nn.sigmoid(zz)
        ybuf[j, sl, :] = y.astype(jnp.bfloat16)
        f_copy(c, j).start()

    def small_grad(c, j):
        sl = pl.ds(pl.multiple_of(c * chunk, chunk), chunk)
        z = zbuf[j, sl, :]
        sig = jax.nn.sigmoid(z)
        dz = dyin[j, sl, :].astype(jnp.float32) * sig * (1.0 + z * (1.0 - sig))
        q_ref[sl, pl.ds(j * cols, cols)] = (dz * inv).astype(jnp.bfloat16)

    def back_project(c, j):
        sl = pl.ds(pl.multiple_of(c * chunk, chunk), chunk)
        q = q_ref[sl, pl.ds(j * cols, cols)]
        for k in range(n_rep):
            du = jnp.dot(q, turned[j, pl.ds(0, cols), pl.ds(k * cols, cols)], preferred_element_type=jnp.float32)
            dubuf[k] = du if j == 0 else dubuf[k] + du

    def emit_back(c):
        sl = pl.ds(pl.multiple_of(c * chunk, chunk), chunk)
        scale = rbuf[sl, :]
        dot_sum = jnp.zeros((chunk, 1), jnp.float32)
        for k in range(n_rep):
            normed = xin[k, sl, :].astype(jnp.float32) * scale
            dot_sum += jnp.sum(dubuf[k] * normed, axis=-1, keepdims=True)
        mean = dot_sum * (1.0 / width)
        for k in range(n_rep):
            normed = xin[k, sl, :].astype(jnp.float32) * scale
            dx = dyin[k, sl, :].astype(jnp.float32) + scale * (dubuf[k] - normed * mean)
            dxbuf[k, sl, :] = dx.astype(jnp.bfloat16)
            b_copy(c, k).start()
        for i in range(2):
            act_store(c, i).start()

    middle = (sec > 0) & (sec < last)

    @pl.when(sec == 0)
    def _():
        @pl.loop(0, n_chunks)
        def _(c):
            for j in range(n_rep):
                emit(c, j)

    @pl.when(middle)
    def _():
        @pl.loop(0, n_chunks)
        def _(c):
            section_input(c)
            for j in range(n_rep):
                project(c, j)
                emit(c, j)

    def rs_add(step, part, mask):
        rs_send_copy(part, step - 1, mask ^ orders[part][step - 1],
                     landed.at[part, 0]).wait_recv()
        at = kept(part, 1).index(mask)
        if step == 1:
            local_copy(part, mask).wait()
        if step == 1 and not mask:
            now_load(part).wait()
        pieces = 4
        piece = half // pieces
        for i in range(pieces):
            ps = pl.ds(i * piece, piece)
            total = landed[part, slot_of(part, step - 1, mask), ps, :].astype(jnp.float32)
            if step == 1:
                total = local[part, at, ps, :].astype(jnp.float32) + total
            elif mask:
                total = local[part, at, ps, :].astype(jnp.float32) + total
            if mask:
                local[part, at, ps, :] = total.astype(jnp.bfloat16)
            else:
                held = pl.ds(part * half + i * piece, piece)
                wf[held, :] = wf[held, :] - rate * total
        if not mask and step == len(bits) - 1:
            base_store(part).start()
        if mask & orders[part][step]:
            rs_send_copy(part, step, mask, local.at[part, at]).start()

    def rs_middle(first):
        for step in range(1, len(bits)):
            for index in range(len(kept(0, step))):
                for part in range(2):
                    mask = ordered(part, step)[index]
                    if first == (step == 1 and mask & orders[part][1] > 0):
                        rs_add(step, part, mask)

    @pl.when(odd & (sec < early))
    def _():
        turn()

    @pl.when(jnp.logical_not(odd) & (sec < early))
    def _():
        pl.semaphore_wait(back, 1)
        rs_start(0)

    @pl.when(sec < early)
    def _():
        rs_middle(True)

    @pl.when(sec < 2)
    def _():
        rs_middle(False)

    @pl.when(sec == 0)
    def _():
        @pl.loop(0, n_chunks)
        def _(c):
            for j in range(n_rep):
                b_copy(c, j).wait_recv()
                small_grad(c, j)
            for i in range(2):
                act_store(c, i).start()

    @pl.when(middle)
    def _():
        @pl.loop(0, n_chunks)
        def _(c):
            for j in range(n_rep):
                b_copy(c, j).wait_recv()
                small_grad(c, j)
                back_project(c, j)
            emit_back(c)

    @pl.when(sec == last)
    def _():
        @pl.loop(0, n_chunks)
        def _(c):
            section_input(c)
            for j in range(n_rep):
                project(c, j)
            for j in range(n_rep):
                small_grad(c, j)
                back_project(c, j)
            emit_back(c)

    @pl.when(sec >= early)
    def _():
        rs_middle(True)

    @pl.when(sec >= 2)
    def _():
        rs_middle(False)

    final = len(bits) - 1
    for part in range(2):
        rs_send_copy(part, final, orders[part][final], local.at[part, 0]).wait_recv()
    @pl.when(sec == 0)
    def _():
        for part in range(2):
            for mask in range(1, n_rep):
                z_copy(part, mask).wait_send()

    for part in range(2):
        for step in range(len(bits)):
            for mask in kept(part, step + 1):
                rs_send_copy(part, step, mask ^ orders[part][step], local.at[part, 0]).wait_send()

    for part in range(2):
        base_store(part).wait()

    @pl.loop(0, n_chunks)
    def _(c):
        for i in range(2):
            act_store(c, i).wait()

    @pl.when(sec < last)
    def _():
        @pl.loop(0, n_chunks)
        def _(c):
            for j in range(n_rep):
                f_copy(c, j).wait_send()

    @pl.when(sec > 0)
    def _():
        @pl.loop(0, n_chunks)
        def _(c):
            for j in range(n_rep):
                b_copy(c, j).wait_send()


def finish(rate, u_ref, q_ref, base_ref, far_ref, next_hbm, grad_hbm,
           next_ref, grad_ref, next_sem, grad_sem):
    count, tile = next_ref.shape[:2]

    def next_store(t):
        return pltpu.make_async_copy(
            next_ref.at[t], next_hbm.at[pl.ds(t * tile, tile), :], next_sem.at[t])

    def grad_store(t):
        return pltpu.make_async_copy(
            grad_ref.at[t], grad_hbm.at[pl.ds(t * tile, tile), :], grad_sem.at[t])

    for t in range(count):
        rows = pl.ds(t * tile, tile)
        next_ref[t] = base_ref[rows, :] - rate * far_ref[rows, :].astype(jnp.float32)
        next_store(t).start()
        grad_ref[t] = lax.dot_general(
            u_ref[:, rows], q_ref[...], (((0,), (0,)), ((), ())),
            preferred_element_type=jnp.float32).astype(jnp.bfloat16)
        grad_store(t).start()
    for t in range(count):
        grad_store(t).wait()
        next_store(t).wait()


def body(inputs, cotangent, w_prev, w_now, grads_prev):
    sections = lax.axis_size("section")
    n_rep = lax.axis_size("dp")
    micro, tok_mb, width = inputs.shape
    rows = micro * tok_mb
    cols = width // n_rep
    half = width // 2
    chunk = tok_mb // SPLIT
    n_chunks = rows // chunk
    any_spec = pl.BlockSpec(memory_space=pl.ANY)
    bf16, f32 = jnp.bfloat16, jnp.float32
    dma = pltpu.SemaphoreType.DMA
    rate = learn_rate / n_rep
    upper, small, base, far = pl.pallas_call(
        functools.partial(relay, n_rep, sections, chunk, rate),
        out_shape=(
            jax.ShapeDtypeStruct((rows, width), bf16),
            jax.ShapeDtypeStruct((rows, width), bf16),
            jax.ShapeDtypeStruct((width, cols), f32),
            jax.ShapeDtypeStruct((width, cols), bf16),
        ),
        in_specs=[any_spec] * 5,
        out_specs=(any_spec,) * 4,
        scratch_shapes=[
            pltpu.VMEM((rows, width), bf16),
            pltpu.VMEM((rows, width), bf16),
            pltpu.VMEM((width, cols), f32),
            pltpu.VMEM((n_rep, width, cols), bf16),
            pltpu.VMEM((n_rep, max(cols, rows), width), bf16),
            pltpu.VMEM((n_rep, rows, cols), bf16),
            pltpu.VMEM((n_rep, rows, cols), bf16),
            pltpu.VMEM((n_rep, rows, cols), bf16),
            pltpu.VMEM((n_rep, rows, cols), bf16),
            pltpu.VMEM((n_rep, rows, cols), f32),
            pltpu.VMEM((rows, 1), f32),
            pltpu.VMEM((n_rep, chunk, cols), f32),
            pltpu.VMEM((2, n_rep // 2, half, cols), bf16),
            pltpu.VMEM((2, max(1, n_rep - 2), half, cols), bf16),
            dma((2,)), dma((n_rep,)), dma((n_rep,)), dma((2, n_rep // 2)),
            dma((2, n_rep)), dma((2, n_rep)),
            dma((2, n_rep)), dma((2, n_rep)),
            dma((n_chunks, n_rep)), dma((n_chunks, n_rep)),
            dma((n_chunks, n_rep)), dma((n_chunks, n_rep)),
            dma((2, n_rep)), dma((2, n_rep)),
            dma((2,)), dma((2,)), dma((2, n_chunks)),
            pltpu.SemaphoreType.REGULAR, pltpu.SemaphoreType.REGULAR,
        ],
        compiler_params=pltpu.CompilerParams(
            collective_id=0, has_side_effects=True, vmem_limit_bytes=40 * 1024 * 1024
        ),
        name="relay",
    )(*(pltpu.with_memory_space_constraint(array, pltpu.HBM) for array in (
        inputs.reshape(rows, width), cotangent.reshape(rows, width), w_prev[0], grads_prev[0, 0], w_now[0])))
    count = 8
    tile = width // count
    w_next, grads_next = pl.pallas_call(
        functools.partial(finish, rate),
        out_shape=(
            jax.ShapeDtypeStruct((width, cols), f32),
            jax.ShapeDtypeStruct((width, width), bf16),
        ),
        in_specs=[pl.BlockSpec(memory_space=pltpu.VMEM)] * 4,
        out_specs=(any_spec,) * 2,
        scratch_shapes=[
            pltpu.VMEM((count, tile, cols), f32),
            pltpu.VMEM((count, tile, width), bf16),
            dma((count,)), dma((count,)),
        ],
        compiler_params=pltpu.CompilerParams(vmem_limit_bytes=24 * 1024 * 1024),
        name="finish",
    )(upper, small, base, far)
    return (w_next[None], grads_next[None, None])


def solution(mesh):
    return jax.shard_map(
        body,
        mesh=mesh,
        in_specs=(
            P(None, "dp", None),
            P(None, "dp", None),
            P("section", None, "dp"),
            P("section", None, "dp"),
            P("dp", "section", None, None),
        ),
        out_specs=(P("section", None, "dp"), P("dp", "section", None, None)),
        check_vma=False,
    )
```

```python
import functools

import jax
import jax.numpy as jnp
from jax import lax
from jax.experimental import pallas as pl
from jax.experimental.pallas import tpu as pltpu
from jax.sharding import PartitionSpec as P

norm_eps = 1e-06
learn_rate = 1.0
MESH = pl.DeviceIdType.MESH
SPLIT = 2
SHARE = 8


def flipped(me, mask):
    out, bit, left = me, 1, mask
    while left:
        if left & 1:
            out = out + bit * (1 - 2 * ((me // bit) % 2))
        left >>= 1
        bit <<= 1
    return out


def spans(order):
    masks = [0]
    for bit in order:
        masks = masks + [mask ^ bit for mask in masks]
    return masks


def relay(n_rep, sections, chunk, rate, x_hbm, cot_hbm, w_hbm, g_hbm, now_hbm,
          u_hbm, q_hbm, base_hbm, far_hbm,
          u_ref, q_ref, wf, weight, turned, xin, dyin, ybuf, dxbuf, zbuf, rbuf, dubuf, local, landed,
          load_sem, x_sem, cot_sem, local_sem,
          ag_send, ag_recv, rs_send, rs_recv, f_send, f_recv, b_send, b_recv,
          z_send, z_recv, now_sem, base_sem, act_sem,
          stage, via_send, stage_recv, hop_send, via_recv, gate, back):
    me = lax.axis_index("dp")
    sec = lax.axis_index("section")
    last = sections - 1
    rows, width = x_hbm.shape
    cols = width // n_rep
    half = width // 2
    n_chunks = rows // chunk
    inv = width ** (-0.5)
    fill = half // 4
    share = half // SHARE
    others = range(sections // 2 - 1)
    lent = (sec % 2) * ((sec + sections - 3) // sections)
    bits = [1 << i for i in range(n_rep.bit_length() - 1)]
    orders = (bits, bits[::-1])

    for part in range(2):
        sl = pl.ds(part * half, half)
        copy = pltpu.make_async_copy(w_hbm.at[sl, :], wf.at[sl, :], load_sem.at[part])
        copy.start()

    def x_load(j):
        return pltpu.make_async_copy(
            x_hbm.at[:, pl.ds(j * cols, cols)], xin.at[j], x_sem.at[j])

    def cot_load(j):
        return pltpu.make_async_copy(
            cot_hbm.at[:, pl.ds(j * cols, cols)], dyin.at[j], cot_sem.at[j])

    @pl.when(sec == 0)
    def _():
        for j in range(n_rep):
            x_load(j).start()

    @pl.when(sec == last)
    def _():
        for j in range(n_rep):
            cot_load(j).start()

    def g_block(part, mask):
        at = pl.multiple_of(flipped(me, mask) * cols, cols)
        return g_hbm.at[pl.ds(part * half, half), pl.ds(at, cols)]

    barrier = pltpu.get_barrier_semaphore()
    for mask in range(1, n_rep):
        pl.semaphore_signal(barrier, inc=1, device_id={"dp": flipped(me, mask)}, device_id_type=MESH)

    @pl.when(sec > 0)
    def _():
        pl.semaphore_signal(barrier, inc=1, device_id={"section": sec - 1}, device_id_type=MESH)

    @pl.when(sec < last)
    def _():
        pl.semaphore_signal(barrier, inc=1, device_id={"section": sec + 1}, device_id_type=MESH)

    firsts = sorted({orders[0][0], orders[1][0]})

    @pl.when(sec == 1)
    def _():
        for index in others:
            for bit in firsts:
                pl.semaphore_signal(
                    barrier, inc=1, device_id={"dp": flipped(me, bit), "section": 2 * index + 3},
                    device_id_type=MESH)

    @pl.when(lent == 1)
    def _():
        pl.semaphore_signal(barrier, inc=1, device_id={"section": 1}, device_id_type=MESH)

    neighbours = (sec + last) // sections + (2 * last - sec) // sections
    helpers = lent * len(firsts) + (sec % 2) * (1 - lent) * len(others)
    pl.semaphore_wait(barrier, n_rep - 1 + neighbours + helpers)

    def piece_of(tokens, part, mask):
        if tokens:
            return turned.at[flipped(me, mask), pl.ds(part * (rows // 2), rows // 2), :]
        return weight.at[flipped(me, mask), pl.ds(part * half, half), :]

    def ag_copy(tokens, part, mask, bit):
        ref = piece_of(tokens, part, mask)
        return pltpu.make_async_remote_copy(
            src_ref=ref, dst_ref=ref,
            send_sem=ag_send.at[part, mask ^ bit], recv_sem=ag_recv.at[part, mask ^ bit],
            device_id={"dp": flipped(me, bit)}, device_id_type=MESH)

    def ag_arrival(tokens, part, mask):
        ref = piece_of(tokens, part, mask)
        return pltpu.make_async_remote_copy(
            src_ref=ref, dst_ref=ref,
            send_sem=ag_send.at[part, mask], recv_sem=ag_recv.at[part, mask],
            device_id={"dp": flipped(me, mask)}, device_id_type=MESH)

    def gather(tokens, prepare):
        for part in range(2):
            prepare(part)
            ag_copy(tokens, part, 0, orders[part][0]).start()
        for step in range(1, len(bits)):
            for part in range(2):
                ag_copy(tokens, part, 0, orders[part][step]).start()
        arrived = set()
        for step in range(1, len(bits)):
            for index in range(1, 1 << step):
                for part in range(2):
                    this = spans(orders[part][:step])[index]
                    if (part, this) not in arrived:
                        ag_arrival(tokens, part, this).wait_recv()
                        arrived.add((part, this))
                    ag_copy(tokens, part, this, orders[part][step]).start()
        return arrived

    def gather_sent(tokens, masks):
        for part in range(2):
            for mask in masks:
                ag_copy(tokens, part, 0, mask).wait_send()

    everyone = range(1, n_rep)
    relayed = [mask for mask in everyone if mask not in bits]

    def cast(part):
        pltpu.make_async_copy(
            w_hbm.at[pl.ds(part * half, half), :], wf.at[pl.ds(part * half, half), :],
            load_sem.at[part]).wait()
        piece = half // 4
        for i in range(4):
            sl = pl.ds(part * half + i * piece, piece)
            weight[me, sl, :] = wf[sl, :].astype(jnp.bfloat16)

    def normalise(sl):
        square = jnp.zeros((chunk, 1), jnp.float32)
        for j in range(n_rep):
            x = xin[j, sl, :].astype(jnp.float32)
            square += jnp.sum(x * x, axis=-1, keepdims=True)
        scale = lax.rsqrt(square * (1.0 / width) + norm_eps)
        rbuf[sl, :] = scale
        for j in range(n_rep):
            x = xin[j, sl, :].astype(jnp.float32)
            u_ref[sl, pl.ds(j * cols, cols)] = (x * scale).astype(jnp.bfloat16)

    def z_copy(part, mask):
        sl = pl.ds(part * (rows // 2), rows // 2)
        return pltpu.make_async_remote_copy(
            src_ref=dxbuf.at[mask, sl, :], dst_ref=dyin.at[me, sl, :],
            send_sem=z_send.at[part, mask], recv_sem=z_recv.at[part, mask],
            device_id={"dp": flipped(me, mask)}, device_id_type=MESH)

    def z_arrival(part, mask):
        sl = pl.ds(part * (rows // 2), rows // 2)
        return pltpu.make_async_remote_copy(
            src_ref=dxbuf.at[mask, sl, :], dst_ref=dyin.at[flipped(me, mask), sl, :],
            send_sem=z_send.at[part, mask], recv_sem=z_recv.at[part, mask],
            device_id={"dp": flipped(me, mask)}, device_id_type=MESH)

    odd = lax.rem(sec, 2) == 1

    def rs_send_copy(part, step, mask, source):
        bit = orders[part][step]
        slot = mask ^ bit
        if step == len(bits) - 1:
            target = far_hbm.at[pl.ds(part * half, half), :]
        else:
            target = landed.at[part, slot_of(part, step, slot)]
        return pltpu.make_async_remote_copy(
            src_ref=source, dst_ref=target,
            send_sem=rs_send.at[part, slot_of(part, step, slot)],
            recv_sem=rs_recv.at[part, slot_of(part, step, slot)],
            device_id={"dp": flipped(me, bit)}, device_id_type=MESH)

    def kept(part, step):
        return sorted(spans(orders[part][step:]))

    def ordered(part, step):
        return sorted(kept(part, step), key=lambda mask: (not mask & orders[part][step], mask))

    def slot_of(part, step, mask):
        base = sum(len(kept(part, s + 1)) for s in range(step))
        return base + kept(part, step + 1).index(mask)

    def local_copy(part, mask):
        at = kept(part, 1).index(mask)
        return pltpu.make_async_copy(
            g_block(part, mask), local.at[part, at], local_sem.at[part, at])

    def rs_rows(part, mask, low, high):
        span = pl.ds(low, high - low)
        slot = slot_of(part, 0, mask ^ orders[part][0])
        pltpu.make_async_remote_copy(
            src_ref=g_block(part, mask).at[span, :], dst_ref=landed.at[part, slot, span, :],
            send_sem=rs_send.at[part, slot], recv_sem=rs_recv.at[part, slot],
            device_id={"dp": flipped(me, orders[part][0])}, device_id_type=MESH).start()

    def rs_early():
        for part in range(2):
            rs_rows(part, ordered(part, 1)[-1] ^ orders[part][0], 0, fill)

    def via_out(part):
        mask = ordered(part, 1)[-1] ^ orders[part][0]
        return pltpu.make_async_remote_copy(
            src_ref=g_block(part, mask).at[pl.ds(half - share, share), :],
            dst_ref=stage.at[jnp.maximum(sec // 2 - 1, 0), part],
            send_sem=via_send.at[part], recv_sem=stage_recv.at[jnp.maximum(sec // 2 - 1, 0), part],
            device_id={"dp": flipped(me, orders[part][0]), "section": 1}, device_id_type=MESH)

    def via_hop(index, part):
        slot = slot_of(part, 0, ordered(part, 1)[-1])
        return pltpu.make_async_remote_copy(
            src_ref=stage.at[index, part],
            dst_ref=landed.at[part, slot, pl.ds(half - share, share), :],
            send_sem=hop_send.at[index, part], recv_sem=via_recv.at[part],
            device_id={"section": 2 * index + 3}, device_id_type=MESH)

    def via_stage(index, part):
        return pltpu.make_async_remote_copy(
            src_ref=stage.at[index, part], dst_ref=stage.at[index, part],
            send_sem=hop_send.at[index, part], recv_sem=stage_recv.at[index, part],
            device_id={"section": 2 * index + 3}, device_id_type=MESH)

    def direct(part):
        slot = slot_of(part, 0, ordered(part, 1)[-1])
        span = pl.ds(0, half - share)
        return pltpu.make_async_remote_copy(
            src_ref=landed.at[part, slot, span, :], dst_ref=landed.at[part, slot, span, :],
            send_sem=rs_send.at[part, slot], recv_sem=rs_recv.at[part, slot],
            device_id={"dp": flipped(me, orders[part][0])}, device_id_type=MESH)

    def rs_start(done, high):
        for mask_at in range(n_rep // 2):
            for part in range(2):
                mask = ordered(part, 1)[mask_at] ^ orders[part][0]
                stays = mask_at == n_rep // 2 - 1
                rs_rows(part, mask, done if stays else 0, high if stays else half)
        for part in range(2):
            for mask in ordered(part, 1):
                local_copy(part, mask).start()

    @pl.when(odd & (sec > 1))
    def _():
        rs_early()

    def turn():
        @pl.loop(0, n_rep)
        def _(j):
            for k in range(n_rep):
                span = pl.ds(k * cols, cols)
                turned[j, pl.ds(0, cols), span] = weight[j, span, :].T

    @pl.when(sec == 0)
    def _():
        for j in range(n_rep):
            x_load(j).wait()

        def prepare(part):
            @pl.loop(part * (n_chunks // 2), (part + 1) * (n_chunks // 2))
            def _(c):
                sl = pl.ds(pl.multiple_of(c * chunk, chunk), chunk)
                normalise(sl)
                turned[me, sl, :] = u_ref[sl, :]

        arrived = gather(True, prepare)
        for part in range(2):
            cast(part)
        for mask in range(n_rep):
            for part in range(2):
                if mask and (part, mask) not in arrived:
                    ag_arrival(True, part, mask).wait_recv()
                sl = pl.ds(part * (rows // 2), rows // 2)
                z = jnp.dot(turned[flipped(me, mask), sl, :], weight[me],
                            preferred_element_type=jnp.float32) * inv
                if mask:
                    dxbuf[mask, sl, :] = z.astype(jnp.bfloat16)
                    z_copy(part, mask).start()
                else:
                    zbuf[me, sl, :] = z
        gather_sent(True, everyone)

    @pl.when((sec > 0) & jnp.logical_not(odd))
    def _():
        arrived = gather(False, cast)
        gather_sent(False, bits)
        pl.semaphore_signal(
            gate, inc=1, device_id={"section": jnp.minimum(sec + 1, last)}, device_id_type=MESH)
        gather_sent(False, relayed)
        for part in range(2):
            for mask in range(1, n_rep):
                if (part, mask) not in arrived:
                    ag_arrival(False, part, mask).wait_recv()
        turn()

    early = sections // 2

    @pl.when(odd)
    def _():
        @pl.when(sec > 1)
        def _():
            pl.semaphore_wait(gate, 1)

        arrived = gather(False, cast)

        @pl.when(sec >= 2)
        def _():
            for part in range(2):
                via_out(part).start()
            rs_start(fill, half - share)

        gather_sent(False, everyone)
        pl.semaphore_signal(
            back, inc=1, device_id={"section": jnp.maximum(sec - 1, 0)}, device_id_type=MESH)

        @pl.when(sec == 1)
        def _():
            rs_early()

        @pl.when(sec < 2)
        def _():
            rs_start(fill, half)

        for part in range(2):
            for mask in range(1, n_rep):
                if (part, mask) not in arrived:
                    ag_arrival(False, part, mask).wait_recv()

    @pl.when(odd & (sec >= early))
    def _():
        turn()

    @pl.when(jnp.logical_not(odd) & (sec >= early))
    def _():
        pl.semaphore_wait(back, 1)
        rs_start(0, half)

    def now_load(part):
        sl = pl.ds(part * half, half)
        return pltpu.make_async_copy(now_hbm.at[sl, :], wf.at[sl, :], now_sem.at[part])

    def base_store(part):
        sl = pl.ds(part * half, half)
        return pltpu.make_async_copy(wf.at[sl, :], base_hbm.at[sl, :], base_sem.at[part])

    def act_store(c, i):
        sl = pl.ds(pl.multiple_of(c * chunk, chunk), chunk)
        source, target = ((u_ref, u_hbm), (q_ref, q_hbm))[i]
        return pltpu.make_async_copy(source.at[sl, :], target.at[sl, :], act_sem.at[i, c])

    for part in range(2):
        now_load(part).start()

    def f_copy(c, j):
        sl = pl.ds(pl.multiple_of(c * chunk, chunk), chunk)
        return pltpu.make_async_remote_copy(
            src_ref=ybuf.at[j, sl, :], dst_ref=xin.at[j, sl, :],
            send_sem=f_send.at[c, j], recv_sem=f_recv.at[c, j],
            device_id={"section": jnp.minimum(sec + 1, last)}, device_id_type=MESH)

    def b_copy(c, j):
        sl = pl.ds(pl.multiple_of(c * chunk, chunk), chunk)
        return pltpu.make_async_remote_copy(
            src_ref=dxbuf.at[j, sl, :], dst_ref=dyin.at[j, sl, :],
            send_sem=b_send.at[c, j], recv_sem=b_recv.at[c, j],
            device_id={"section": jnp.maximum(sec - 1, 0)}, device_id_type=MESH)

    @pl.when(sec == 0)
    def _():
        for part in range(2):
            for mask in range(1, n_rep):
                z_arrival(part, mask).wait_recv()
                sl = pl.ds(part * (rows // 2), rows // 2)
                zbuf[flipped(me, mask), sl, :] = dyin[flipped(me, mask), sl, :].astype(jnp.float32)

    @pl.when(sec == last)
    def _():
        for j in range(n_rep):
            cot_load(j).wait()

    def section_input(c):
        for j in range(n_rep):
            f_copy(c, j).wait_recv()
        normalise(pl.ds(pl.multiple_of(c * chunk, chunk), chunk))

    def project(c, j):
        sl = pl.ds(pl.multiple_of(c * chunk, chunk), chunk)
        zbuf[j, sl, :] = jnp.dot(
            u_ref[sl, :], weight[j], preferred_element_type=jnp.float32) * inv

    def emit(c, j):
        sl = pl.ds(pl.multiple_of(c * chunk, chunk), chunk)
        zz = zbuf[j, sl, :]
        y = xin[j, sl, :].astype(jnp.float32) + zz * jax.nn.sigmoid(zz)
        ybuf[j, sl, :] = y.astype(jnp.bfloat16)
        f_copy(c, j).start()

    def small_grad(c, j):
        sl = pl.ds(pl.multiple_of(c * chunk, chunk), chunk)
        z = zbuf[j, sl, :]
        sig = jax.nn.sigmoid(z)
        dz = dyin[j, sl, :].astype(jnp.float32) * sig * (1.0 + z * (1.0 - sig))
        q_ref[sl, pl.ds(j * cols, cols)] = (dz * inv).astype(jnp.bfloat16)

    def back_project(c, j):
        sl = pl.ds(pl.multiple_of(c * chunk, chunk), chunk)
        q = q_ref[sl, pl.ds(j * cols, cols)]
        for k in range(n_rep):
            du = jnp.dot(q, turned[j, pl.ds(0, cols), pl.ds(k * cols, cols)], preferred_element_type=jnp.float32)
            dubuf[k] = du if j == 0 else dubuf[k] + du

    def emit_back(c):
        sl = pl.ds(pl.multiple_of(c * chunk, chunk), chunk)
        scale = rbuf[sl, :]
        dot_sum = jnp.zeros((chunk, 1), jnp.float32)
        for k in range(n_rep):
            normed = xin[k, sl, :].astype(jnp.float32) * scale
            dot_sum += jnp.sum(dubuf[k] * normed, axis=-1, keepdims=True)
        mean = dot_sum * (1.0 / width)
        for k in range(n_rep):
            normed = xin[k, sl, :].astype(jnp.float32) * scale
            dx = dyin[k, sl, :].astype(jnp.float32) + scale * (dubuf[k] - normed * mean)
            dxbuf[k, sl, :] = dx.astype(jnp.bfloat16)
            b_copy(c, k).start()
        for i in range(2):
            act_store(c, i).start()

    middle = (sec > 0) & (sec < last)

    @pl.when(sec == 0)
    def _():
        @pl.loop(0, n_chunks)
        def _(c):
            for j in range(n_rep):
                emit(c, j)

    @pl.when(middle)
    def _():
        @pl.loop(0, n_chunks)
        def _(c):
            section_input(c)
            for j in range(n_rep):
                project(c, j)
                emit(c, j)

    def rs_add(step, part, mask):
        arrival = rs_send_copy(part, step - 1, mask ^ orders[part][step - 1], landed.at[part, 0])
        if step == 1 and mask == ordered(part, 1)[-1]:
            @pl.when(lent == 1)
            def _():
                direct(part).wait_recv()
                via_hop(0, part).wait_recv()

            @pl.when(lent == 0)
            def _():
                arrival.wait_recv()
        else:
            arrival.wait_recv()
        at = kept(part, 1).index(mask)
        if step == 1:
            local_copy(part, mask).wait()
        if step == 1 and not mask:
            now_load(part).wait()
        pieces = 4
        piece = half // pieces
        for i in range(pieces):
            ps = pl.ds(i * piece, piece)
            total = landed[part, slot_of(part, step - 1, mask), ps, :].astype(jnp.float32)
            if step == 1:
                total = local[part, at, ps, :].astype(jnp.float32) + total
            elif mask:
                total = local[part, at, ps, :].astype(jnp.float32) + total
            if mask:
                local[part, at, ps, :] = total.astype(jnp.bfloat16)
            else:
                held = pl.ds(part * half + i * piece, piece)
                wf[held, :] = wf[held, :] - rate * total
        if not mask and step == len(bits) - 1:
            base_store(part).start()
        if mask & orders[part][step]:
            rs_send_copy(part, step, mask, local.at[part, at]).start()

    def rs_middle(first):
        for step in range(1, len(bits)):
            for index in range(len(kept(0, step))):
                for part in range(2):
                    mask = ordered(part, step)[index]
                    if first == (step == 1 and mask & orders[part][1] > 0):
                        rs_add(step, part, mask)

    @pl.when(odd & (sec < early))
    def _():
        turn()

    @pl.when(jnp.logical_not(odd) & (sec < early))
    def _():
        pl.semaphore_wait(back, 1)
        rs_start(0, half)

    @pl.when(sec < early)
    def _():
        rs_middle(True)

    @pl.when(sec == 1)
    def _():
        for index in others:
            for part in range(2):
                via_stage(index, part).wait_recv()
                via_hop(index, part).start()

    @pl.when(sec == 0)
    def _():
        @pl.loop(0, n_chunks)
        def _(c):
            for j in range(n_rep):
                b_copy(c, j).wait_recv()
                small_grad(c, j)
            for i in range(2):
                act_store(c, i).start()

    @pl.when(middle)
    def _():
        @pl.loop(0, n_chunks)
        def _(c):
            for j in range(n_rep):
                b_copy(c, j).wait_recv()
                small_grad(c, j)
                back_project(c, j)
            emit_back(c)

            @pl.when((c == n_chunks // 2 - 1) & (sec >= early) & (sec < sections - 2))
            def _():
                rs_middle(True)

    @pl.when(sec == last)
    def _():
        @pl.loop(0, n_chunks)
        def _(c):
            section_input(c)
            for j in range(n_rep):
                project(c, j)
            for j in range(n_rep):
                small_grad(c, j)
                back_project(c, j)
            emit_back(c)

    @pl.when(sec >= sections - 2)
    def _():
        rs_middle(True)

    rs_middle(False)

    final = len(bits) - 1
    for part in range(2):
        rs_send_copy(part, final, orders[part][final], local.at[part, 0]).wait_recv()
    @pl.when(sec == 0)
    def _():
        for part in range(2):
            for mask in range(1, n_rep):
                z_copy(part, mask).wait_send()

    for part in range(2):
        for step in range(len(bits)):
            for mask in kept(part, step + 1):
                sent = rs_send_copy(part, step, mask ^ orders[part][step], local.at[part, 0])
                if step == 0 and mask == ordered(part, 1)[-1]:
                    @pl.when(lent == 1)
                    def _():
                        direct(part).wait_send()
                        via_out(part).wait_send()

                    @pl.when(lent == 0)
                    def _():
                        sent.wait_send()
                else:
                    sent.wait_send()

    @pl.when(sec == 1)
    def _():
        for index in others:
            for part in range(2):
                via_hop(index, part).wait_send()

    for part in range(2):
        base_store(part).wait()

    @pl.loop(0, n_chunks)
    def _(c):
        for i in range(2):
            act_store(c, i).wait()

    @pl.when(sec < last)
    def _():
        @pl.loop(0, n_chunks)
        def _(c):
            for j in range(n_rep):
                f_copy(c, j).wait_send()

    @pl.when(sec > 0)
    def _():
        @pl.loop(0, n_chunks)
        def _(c):
            for j in range(n_rep):
                b_copy(c, j).wait_send()


def finish(rate, u_ref, q_ref, base_ref, far_ref, next_hbm, grad_hbm,
           next_ref, grad_ref, next_sem, grad_sem):
    count, tile = next_ref.shape[:2]

    def next_store(t):
        return pltpu.make_async_copy(
            next_ref.at[t], next_hbm.at[pl.ds(t * tile, tile), :], next_sem.at[t])

    def grad_store(t):
        return pltpu.make_async_copy(
            grad_ref.at[t], grad_hbm.at[pl.ds(t * tile, tile), :], grad_sem.at[t])

    for t in range(count):
        rows = pl.ds(t * tile, tile)
        next_ref[t] = base_ref[rows, :] - rate * far_ref[rows, :].astype(jnp.float32)
        next_store(t).start()
        grad_ref[t] = lax.dot_general(
            u_ref[:, rows], q_ref[...], (((0,), (0,)), ((), ())),
            preferred_element_type=jnp.float32).astype(jnp.bfloat16)
        grad_store(t).start()
    for t in range(count):
        grad_store(t).wait()
        next_store(t).wait()


def body(inputs, cotangent, w_prev, w_now, grads_prev):
    sections = lax.axis_size("section")
    n_rep = lax.axis_size("dp")
    micro, tok_mb, width = inputs.shape
    rows = micro * tok_mb
    cols = width // n_rep
    half = width // 2
    chunk = tok_mb // SPLIT
    n_chunks = rows // chunk
    any_spec = pl.BlockSpec(memory_space=pl.ANY)
    bf16, f32 = jnp.bfloat16, jnp.float32
    dma = pltpu.SemaphoreType.DMA
    rate = learn_rate / n_rep
    upper, small, base, far = pl.pallas_call(
        functools.partial(relay, n_rep, sections, chunk, rate),
        out_shape=(
            jax.ShapeDtypeStruct((rows, width), bf16),
            jax.ShapeDtypeStruct((rows, width), bf16),
            jax.ShapeDtypeStruct((width, cols), f32),
            jax.ShapeDtypeStruct((width, cols), bf16),
        ),
        in_specs=[any_spec] * 5,
        out_specs=(any_spec,) * 4,
        scratch_shapes=[
            pltpu.VMEM((rows, width), bf16),
            pltpu.VMEM((rows, width), bf16),
            pltpu.VMEM((width, cols), f32),
            pltpu.VMEM((n_rep, width, cols), bf16),
            pltpu.VMEM((n_rep, max(cols, rows), width), bf16),
            pltpu.VMEM((n_rep, rows, cols), bf16),
            pltpu.VMEM((n_rep, rows, cols), bf16),
            pltpu.VMEM((n_rep, rows, cols), bf16),
            pltpu.VMEM((n_rep, rows, cols), bf16),
            pltpu.VMEM((n_rep, rows, cols), f32),
            pltpu.VMEM((rows, 1), f32),
            pltpu.VMEM((n_rep, chunk, cols), f32),
            pltpu.VMEM((2, n_rep // 2, half, cols), bf16),
            pltpu.VMEM((2, max(1, n_rep - 2), half, cols), bf16),
            dma((2,)), dma((n_rep,)), dma((n_rep,)), dma((2, n_rep // 2)),
            dma((2, n_rep)), dma((2, n_rep)),
            dma((2, n_rep)), dma((2, n_rep)),
            dma((n_chunks, n_rep)), dma((n_chunks, n_rep)),
            dma((n_chunks, n_rep)), dma((n_chunks, n_rep)),
            dma((2, n_rep)), dma((2, n_rep)),
            dma((2,)), dma((2,)), dma((2, n_chunks)),
            pltpu.VMEM((sections // 2 - 1, 2, half // SHARE, cols), bf16),
            dma((2,)), dma((sections // 2 - 1, 2)), dma((sections // 2 - 1, 2)), dma((2,)),
            pltpu.SemaphoreType.REGULAR, pltpu.SemaphoreType.REGULAR,
        ],
        compiler_params=pltpu.CompilerParams(
            collective_id=0, has_side_effects=True, vmem_limit_bytes=40 * 1024 * 1024
        ),
        name="relay",
    )(*(pltpu.with_memory_space_constraint(array, pltpu.HBM) for array in (
        inputs.reshape(rows, width), cotangent.reshape(rows, width), w_prev[0], grads_prev[0, 0], w_now[0])))
    count = 8
    tile = width // count
    w_next, grads_next = pl.pallas_call(
        functools.partial(finish, rate),
        out_shape=(
            jax.ShapeDtypeStruct((width, cols), f32),
            jax.ShapeDtypeStruct((width, width), bf16),
        ),
        in_specs=[pl.BlockSpec(memory_space=pltpu.VMEM)] * 4,
        out_specs=(any_spec,) * 2,
        scratch_shapes=[
            pltpu.VMEM((count, tile, cols), f32),
            pltpu.VMEM((count, tile, width), bf16),
            dma((count,)), dma((count,)),
        ],
        compiler_params=pltpu.CompilerParams(vmem_limit_bytes=24 * 1024 * 1024),
        name="finish",
    )(upper, small, base, far)
    return (w_next[None], grads_next[None, None])


def solution(mesh):
    return jax.shard_map(
        body,
        mesh=mesh,
        in_specs=(
            P(None, "dp", None),
            P(None, "dp", None),
            P("section", None, "dp"),
            P("section", None, "dp"),
            P("dp", "section", None, None),
        ),
        out_specs=(P("section", None, "dp"), P("dp", "section", None, None)),
        check_vma=False,
    )
```

```python
import functools

import jax
import jax.numpy as jnp
from jax import lax
from jax.experimental import pallas as pl
from jax.experimental.pallas import tpu as pltpu
from jax.sharding import PartitionSpec as P

norm_eps = 1e-06
learn_rate = 1.0
MESH = pl.DeviceIdType.MESH
SPLIT = 2
SHARE = 5


def flipped(me, mask):
    out, bit, left = me, 1, mask
    while left:
        if left & 1:
            out = out + bit * (1 - 2 * ((me // bit) % 2))
        left >>= 1
        bit <<= 1
    return out


def spans(order):
    masks = [0]
    for bit in order:
        masks = masks + [mask ^ bit for mask in masks]
    return masks


def relay(n_rep, sections, chunk, rate, x_hbm, cot_hbm, w_hbm, g_hbm, now_hbm,
          u_hbm, q_hbm, base_hbm, far_hbm,
          u_ref, q_ref, wf, weight, turned, xin, dyin, ybuf, dxbuf, zbuf, rbuf, dubuf, local, landed,
          load_sem, x_sem, cot_sem, local_sem,
          ag_send, ag_recv, rs_send, rs_recv, f_send, f_recv, b_send, b_recv,
          z_send, z_recv, now_sem, base_sem, act_sem,
          stage, via_send, stage_recv, hop_send, via_recv, gate, back):
    me = lax.axis_index("dp")
    sec = lax.axis_index("section")
    last = sections - 1
    rows, width = x_hbm.shape
    cols = width // n_rep
    half = width // 2
    n_chunks = rows // chunk
    inv = width ** (-0.5)
    fill = half // 4
    share = half * SHARE // 32
    others = range(sections // 2 - 1)
    lent = (sec % 2) * ((sec + sections - 3) // sections)
    bits = [1 << i for i in range(n_rep.bit_length() - 1)]
    orders = (bits, bits[::-1])

    for part in range(2):
        sl = pl.ds(part * half, half)
        copy = pltpu.make_async_copy(w_hbm.at[sl, :], wf.at[sl, :], load_sem.at[part])
        copy.start()

    def x_load(j):
        return pltpu.make_async_copy(
            x_hbm.at[:, pl.ds(j * cols, cols)], xin.at[j], x_sem.at[j])

    def cot_load(j):
        return pltpu.make_async_copy(
            cot_hbm.at[:, pl.ds(j * cols, cols)], dyin.at[j], cot_sem.at[j])

    @pl.when(sec == 0)
    def _():
        for j in range(n_rep):
            x_load(j).start()

    @pl.when(sec == last)
    def _():
        for j in range(n_rep):
            cot_load(j).start()

    def g_block(part, mask):
        at = pl.multiple_of(flipped(me, mask) * cols, cols)
        return g_hbm.at[pl.ds(part * half, half), pl.ds(at, cols)]

    barrier = pltpu.get_barrier_semaphore()
    for mask in range(1, n_rep):
        pl.semaphore_signal(barrier, inc=1, device_id={"dp": flipped(me, mask)}, device_id_type=MESH)

    @pl.when(sec > 0)
    def _():
        pl.semaphore_signal(barrier, inc=1, device_id={"section": sec - 1}, device_id_type=MESH)

    @pl.when(sec < last)
    def _():
        pl.semaphore_signal(barrier, inc=1, device_id={"section": sec + 1}, device_id_type=MESH)

    firsts = sorted({orders[0][0], orders[1][0]})

    @pl.when(sec == 1)
    def _():
        for index in others:
            for bit in firsts:
                pl.semaphore_signal(
                    barrier, inc=1, device_id={"dp": flipped(me, bit), "section": 2 * index + 3},
                    device_id_type=MESH)

    @pl.when(lent == 1)
    def _():
        pl.semaphore_signal(barrier, inc=1, device_id={"section": 1}, device_id_type=MESH)

    neighbours = (sec + last) // sections + (2 * last - sec) // sections
    helpers = lent * len(firsts) + (sec % 2) * (1 - lent) * len(others)
    pl.semaphore_wait(barrier, n_rep - 1 + neighbours + helpers)

    def piece_of(tokens, part, mask):
        if tokens:
            return turned.at[flipped(me, mask), pl.ds(part * (rows // 2), rows // 2), :]
        return weight.at[flipped(me, mask), pl.ds(part * half, half), :]

    def ag_copy(tokens, part, mask, bit):
        ref = piece_of(tokens, part, mask)
        return pltpu.make_async_remote_copy(
            src_ref=ref, dst_ref=ref,
            send_sem=ag_send.at[part, mask ^ bit], recv_sem=ag_recv.at[part, mask ^ bit],
            device_id={"dp": flipped(me, bit)}, device_id_type=MESH)

    def ag_arrival(tokens, part, mask):
        ref = piece_of(tokens, part, mask)
        return pltpu.make_async_remote_copy(
            src_ref=ref, dst_ref=ref,
            send_sem=ag_send.at[part, mask], recv_sem=ag_recv.at[part, mask],
            device_id={"dp": flipped(me, mask)}, device_id_type=MESH)

    def gather(tokens, prepare):
        for part in range(2):
            prepare(part)
            ag_copy(tokens, part, 0, orders[part][0]).start()
        for step in range(1, len(bits)):
            for part in range(2):
                ag_copy(tokens, part, 0, orders[part][step]).start()
        arrived = set()
        for step in range(1, len(bits)):
            for index in range(1, 1 << step):
                for part in range(2):
                    this = spans(orders[part][:step])[index]
                    if (part, this) not in arrived:
                        ag_arrival(tokens, part, this).wait_recv()
                        arrived.add((part, this))
                    ag_copy(tokens, part, this, orders[part][step]).start()
        return arrived

    def gather_sent(tokens, masks):
        for part in range(2):
            for mask in masks:
                ag_copy(tokens, part, 0, mask).wait_send()

    everyone = range(1, n_rep)
    relayed = [mask for mask in everyone if mask not in bits]

    def cast(part):
        pltpu.make_async_copy(
            w_hbm.at[pl.ds(part * half, half), :], wf.at[pl.ds(part * half, half), :],
            load_sem.at[part]).wait()
        piece = half // 4
        for i in range(4):
            sl = pl.ds(part * half + i * piece, piece)
            weight[me, sl, :] = wf[sl, :].astype(jnp.bfloat16)

    def normalise(sl):
        square = jnp.zeros((chunk, 1), jnp.float32)
        for j in range(n_rep):
            x = xin[j, sl, :].astype(jnp.float32)
            square += jnp.sum(x * x, axis=-1, keepdims=True)
        scale = lax.rsqrt(square * (1.0 / width) + norm_eps)
        rbuf[sl, :] = scale
        for j in range(n_rep):
            x = xin[j, sl, :].astype(jnp.float32)
            u_ref[sl, pl.ds(j * cols, cols)] = (x * scale).astype(jnp.bfloat16)

    def z_copy(part, mask):
        sl = pl.ds(part * (rows // 2), rows // 2)
        return pltpu.make_async_remote_copy(
            src_ref=dxbuf.at[mask, sl, :], dst_ref=dyin.at[me, sl, :],
            send_sem=z_send.at[part, mask], recv_sem=z_recv.at[part, mask],
            device_id={"dp": flipped(me, mask)}, device_id_type=MESH)

    def z_arrival(part, mask):
        sl = pl.ds(part * (rows // 2), rows // 2)
        return pltpu.make_async_remote_copy(
            src_ref=dxbuf.at[mask, sl, :], dst_ref=dyin.at[flipped(me, mask), sl, :],
            send_sem=z_send.at[part, mask], recv_sem=z_recv.at[part, mask],
            device_id={"dp": flipped(me, mask)}, device_id_type=MESH)

    odd = lax.rem(sec, 2) == 1

    def rs_send_copy(part, step, mask, source):
        bit = orders[part][step]
        slot = mask ^ bit
        if step == len(bits) - 1:
            target = far_hbm.at[pl.ds(part * half, half), :]
        else:
            target = landed.at[part, slot_of(part, step, slot)]
        return pltpu.make_async_remote_copy(
            src_ref=source, dst_ref=target,
            send_sem=rs_send.at[part, slot_of(part, step, slot)],
            recv_sem=rs_recv.at[part, slot_of(part, step, slot)],
            device_id={"dp": flipped(me, bit)}, device_id_type=MESH)

    def kept(part, step):
        return sorted(spans(orders[part][step:]))

    def ordered(part, step):
        return sorted(kept(part, step), key=lambda mask: (not mask & orders[part][step], mask))

    def slot_of(part, step, mask):
        base = sum(len(kept(part, s + 1)) for s in range(step))
        return base + kept(part, step + 1).index(mask)

    def local_copy(part, mask):
        at = kept(part, 1).index(mask)
        return pltpu.make_async_copy(
            g_block(part, mask), local.at[part, at], local_sem.at[part, at])

    def rs_rows(part, mask, low, high):
        span = pl.ds(low, high - low)
        slot = slot_of(part, 0, mask ^ orders[part][0])
        pltpu.make_async_remote_copy(
            src_ref=g_block(part, mask).at[span, :], dst_ref=landed.at[part, slot, span, :],
            send_sem=rs_send.at[part, slot], recv_sem=rs_recv.at[part, slot],
            device_id={"dp": flipped(me, orders[part][0])}, device_id_type=MESH).start()

    def rs_early():
        for part in range(2):
            rs_rows(part, ordered(part, 1)[-1] ^ orders[part][0], 0, fill)

    def via_out(part):
        mask = ordered(part, 1)[-1] ^ orders[part][0]
        return pltpu.make_async_remote_copy(
            src_ref=g_block(part, mask).at[pl.ds(half - share, share), :],
            dst_ref=stage.at[jnp.maximum(sec // 2 - 1, 0), part],
            send_sem=via_send.at[part], recv_sem=stage_recv.at[jnp.maximum(sec // 2 - 1, 0), part],
            device_id={"dp": flipped(me, orders[part][0]), "section": 1}, device_id_type=MESH)

    def via_hop(index, part):
        slot = slot_of(part, 0, ordered(part, 1)[-1])
        return pltpu.make_async_remote_copy(
            src_ref=stage.at[index, part],
            dst_ref=landed.at[part, slot, pl.ds(half - share, share), :],
            send_sem=hop_send.at[index, part], recv_sem=via_recv.at[part],
            device_id={"section": 2 * index + 3}, device_id_type=MESH)

    def via_stage(index, part):
        return pltpu.make_async_remote_copy(
            src_ref=stage.at[index, part], dst_ref=stage.at[index, part],
            send_sem=hop_send.at[index, part], recv_sem=stage_recv.at[index, part],
            device_id={"section": 2 * index + 3}, device_id_type=MESH)

    def direct(part):
        slot = slot_of(part, 0, ordered(part, 1)[-1])
        span = pl.ds(0, half - share)
        return pltpu.make_async_remote_copy(
            src_ref=landed.at[part, slot, span, :], dst_ref=landed.at[part, slot, span, :],
            send_sem=rs_send.at[part, slot], recv_sem=rs_recv.at[part, slot],
            device_id={"dp": flipped(me, orders[part][0])}, device_id_type=MESH)

    def rs_start(done, high):
        for mask_at in range(n_rep // 2):
            for part in range(2):
                mask = ordered(part, 1)[mask_at] ^ orders[part][0]
                stays = mask_at == n_rep // 2 - 1
                rs_rows(part, mask, done if stays else 0, high if stays else half)
        for part in range(2):
            for mask in ordered(part, 1):
                local_copy(part, mask).start()

    @pl.when(odd & (sec > 1))
    def _():
        rs_early()

    def turn():
        @pl.loop(0, n_rep)
        def _(j):
            for k in range(n_rep):
                span = pl.ds(k * cols, cols)
                turned[j, pl.ds(0, cols), span] = weight[j, span, :].T

    @pl.when(sec == 0)
    def _():
        for j in range(n_rep):
            x_load(j).wait()

        def prepare(part):
            @pl.loop(part * (n_chunks // 2), (part + 1) * (n_chunks // 2))
            def _(c):
                sl = pl.ds(pl.multiple_of(c * chunk, chunk), chunk)
                normalise(sl)
                turned[me, sl, :] = u_ref[sl, :]

        arrived = gather(True, prepare)
        for part in range(2):
            cast(part)
        for mask in range(n_rep):
            for part in range(2):
                if mask and (part, mask) not in arrived:
                    ag_arrival(True, part, mask).wait_recv()
                sl = pl.ds(part * (rows // 2), rows // 2)
                z = jnp.dot(turned[flipped(me, mask), sl, :], weight[me],
                            preferred_element_type=jnp.float32) * inv
                if mask:
                    dxbuf[mask, sl, :] = z.astype(jnp.bfloat16)
                    z_copy(part, mask).start()
                else:
                    zbuf[me, sl, :] = z
        gather_sent(True, everyone)

    @pl.when((sec > 0) & jnp.logical_not(odd))
    def _():
        arrived = gather(False, cast)
        gather_sent(False, bits)
        pl.semaphore_signal(
            gate, inc=1, device_id={"section": jnp.minimum(sec + 1, last)}, device_id_type=MESH)
        gather_sent(False, relayed)
        for part in range(2):
            for mask in range(1, n_rep):
                if (part, mask) not in arrived:
                    ag_arrival(False, part, mask).wait_recv()
        turn()

    early = sections // 2

    @pl.when(odd)
    def _():
        @pl.when(sec > 1)
        def _():
            pl.semaphore_wait(gate, 1)

        arrived = gather(False, cast)

        @pl.when(sec == 1)
        def _():
            rs_early()

        @pl.when(sec >= 2)
        def _():
            for part in range(2):
                via_out(part).start()
            rs_start(fill, half - share)

        gather_sent(False, everyone)
        pl.semaphore_signal(
            back, inc=1, device_id={"section": jnp.maximum(sec - 1, 0)}, device_id_type=MESH)

        @pl.when(sec < 2)
        def _():
            rs_start(fill, half)

        for part in range(2):
            for mask in range(1, n_rep):
                if (part, mask) not in arrived:
                    ag_arrival(False, part, mask).wait_recv()

    @pl.when(odd & (sec >= early))
    def _():
        turn()

    @pl.when(jnp.logical_not(odd) & (sec >= early))
    def _():
        pl.semaphore_wait(back, 1)
        rs_start(0, half)

    def now_load(part):
        sl = pl.ds(part * half, half)
        return pltpu.make_async_copy(now_hbm.at[sl, :], wf.at[sl, :], now_sem.at[part])

    def base_store(part):
        sl = pl.ds(part * half, half)
        return pltpu.make_async_copy(wf.at[sl, :], base_hbm.at[sl, :], base_sem.at[part])

    def act_store(c, i):
        sl = pl.ds(pl.multiple_of(c * chunk, chunk), chunk)
        source, target = ((u_ref, u_hbm), (q_ref, q_hbm))[i]
        return pltpu.make_async_copy(source.at[sl, :], target.at[sl, :], act_sem.at[i, c])

    for part in range(2):
        now_load(part).start()

    def f_copy(c, j):
        sl = pl.ds(pl.multiple_of(c * chunk, chunk), chunk)
        return pltpu.make_async_remote_copy(
            src_ref=ybuf.at[j, sl, :], dst_ref=xin.at[j, sl, :],
            send_sem=f_send.at[c, j], recv_sem=f_recv.at[c, j],
            device_id={"section": jnp.minimum(sec + 1, last)}, device_id_type=MESH)

    def b_copy(c, j):
        sl = pl.ds(pl.multiple_of(c * chunk, chunk), chunk)
        return pltpu.make_async_remote_copy(
            src_ref=dxbuf.at[j, sl, :], dst_ref=dyin.at[j, sl, :],
            send_sem=b_send.at[c, j], recv_sem=b_recv.at[c, j],
            device_id={"section": jnp.maximum(sec - 1, 0)}, device_id_type=MESH)

    @pl.when(sec == 0)
    def _():
        for part in range(2):
            for mask in range(1, n_rep):
                z_arrival(part, mask).wait_recv()
                sl = pl.ds(part * (rows // 2), rows // 2)
                zbuf[flipped(me, mask), sl, :] = dyin[flipped(me, mask), sl, :].astype(jnp.float32)

    @pl.when(sec == last)
    def _():
        for j in range(n_rep):
            cot_load(j).wait()

    def section_input(c):
        for j in range(n_rep):
            f_copy(c, j).wait_recv()
        normalise(pl.ds(pl.multiple_of(c * chunk, chunk), chunk))

    def project(c, j):
        sl = pl.ds(pl.multiple_of(c * chunk, chunk), chunk)
        zbuf[j, sl, :] = jnp.dot(
            u_ref[sl, :], weight[j], preferred_element_type=jnp.float32) * inv

    def emit(c, j):
        sl = pl.ds(pl.multiple_of(c * chunk, chunk), chunk)
        zz = zbuf[j, sl, :]
        y = xin[j, sl, :].astype(jnp.float32) + zz * jax.nn.sigmoid(zz)
        ybuf[j, sl, :] = y.astype(jnp.bfloat16)
        f_copy(c, j).start()

    def small_grad(c, j):
        sl = pl.ds(pl.multiple_of(c * chunk, chunk), chunk)
        z = zbuf[j, sl, :]
        sig = jax.nn.sigmoid(z)
        dz = dyin[j, sl, :].astype(jnp.float32) * sig * (1.0 + z * (1.0 - sig))
        q_ref[sl, pl.ds(j * cols, cols)] = (dz * inv).astype(jnp.bfloat16)

    def back_project(c, j):
        sl = pl.ds(pl.multiple_of(c * chunk, chunk), chunk)
        q = q_ref[sl, pl.ds(j * cols, cols)]
        for k in range(n_rep):
            du = jnp.dot(q, turned[j, pl.ds(0, cols), pl.ds(k * cols, cols)], preferred_element_type=jnp.float32)
            dubuf[k] = du if j == 0 else dubuf[k] + du

    def emit_back(c):
        sl = pl.ds(pl.multiple_of(c * chunk, chunk), chunk)
        scale = rbuf[sl, :]
        dot_sum = jnp.zeros((chunk, 1), jnp.float32)
        for k in range(n_rep):
            normed = xin[k, sl, :].astype(jnp.float32) * scale
            dot_sum += jnp.sum(dubuf[k] * normed, axis=-1, keepdims=True)
        mean = dot_sum * (1.0 / width)
        for k in range(n_rep):
            normed = xin[k, sl, :].astype(jnp.float32) * scale
            dx = dyin[k, sl, :].astype(jnp.float32) + scale * (dubuf[k] - normed * mean)
            dxbuf[k, sl, :] = dx.astype(jnp.bfloat16)
            b_copy(c, k).start()
        for i in range(2):
            act_store(c, i).start()

    middle = (sec > 0) & (sec < last)

    @pl.when(sec == 0)
    def _():
        @pl.loop(0, n_chunks)
        def _(c):
            for j in range(n_rep):
                emit(c, j)

    @pl.when(middle)
    def _():
        @pl.loop(0, n_chunks)
        def _(c):
            section_input(c)
            for j in range(n_rep):
                project(c, j)
                emit(c, j)

    def rs_add(step, part, mask):
        arrival = rs_send_copy(part, step - 1, mask ^ orders[part][step - 1], landed.at[part, 0])
        if step == 1 and mask == ordered(part, 1)[-1]:
            @pl.when(lent == 1)
            def _():
                direct(part).wait_recv()
                via_hop(0, part).wait_recv()

            @pl.when(lent == 0)
            def _():
                arrival.wait_recv()
        else:
            arrival.wait_recv()
        at = kept(part, 1).index(mask)
        if step == 1:
            local_copy(part, mask).wait()
        if step == 1 and not mask:
            now_load(part).wait()
        pieces = 4
        piece = half // pieces
        for i in range(pieces):
            ps = pl.ds(i * piece, piece)
            total = landed[part, slot_of(part, step - 1, mask), ps, :].astype(jnp.float32)
            if step == 1:
                total = local[part, at, ps, :].astype(jnp.float32) + total
            elif mask:
                total = local[part, at, ps, :].astype(jnp.float32) + total
            if mask:
                local[part, at, ps, :] = total.astype(jnp.bfloat16)
            else:
                held = pl.ds(part * half + i * piece, piece)
                wf[held, :] = wf[held, :] - rate * total
        if not mask and step == len(bits) - 1:
            base_store(part).start()
        if mask & orders[part][step]:
            rs_send_copy(part, step, mask, local.at[part, at]).start()

    def rs_middle(first):
        for step in range(1, len(bits)):
            for index in range(len(kept(0, step))):
                for part in range(2):
                    mask = ordered(part, step)[index]
                    if first == (step == 1 and mask & orders[part][1] > 0):
                        rs_add(step, part, mask)

    @pl.when(odd & (sec < early))
    def _():
        turn()

    @pl.when(jnp.logical_not(odd) & (sec < early))
    def _():
        pl.semaphore_wait(back, 1)
        rs_start(0, half)

    @pl.when(sec < early)
    def _():
        rs_middle(True)

    @pl.when(sec == 1)
    def _():
        for index in others:
            for part in range(2):
                via_stage(index, part).wait_recv()
                via_hop(index, part).start()

    @pl.when(sec == 0)
    def _():
        @pl.loop(0, n_chunks)
        def _(c):
            for j in range(n_rep):
                b_copy(c, j).wait_recv()
                small_grad(c, j)
            for i in range(2):
                act_store(c, i).start()

    @pl.when(middle)
    def _():
        @pl.loop(0, n_chunks)
        def _(c):
            for j in range(n_rep):
                b_copy(c, j).wait_recv()
                small_grad(c, j)
                back_project(c, j)
            emit_back(c)

            @pl.when((c == n_chunks // 2 - 1) & (sec >= early) & (sec < sections - 2))
            def _():
                rs_middle(True)

    @pl.when(sec == last)
    def _():
        @pl.loop(0, n_chunks)
        def _(c):
            section_input(c)
            for j in range(n_rep):
                project(c, j)
            for j in range(n_rep):
                small_grad(c, j)
                back_project(c, j)
            emit_back(c)

    @pl.when(sec >= sections - 2)
    def _():
        rs_middle(True)

    rs_middle(False)

    final = len(bits) - 1
    for part in range(2):
        rs_send_copy(part, final, orders[part][final], local.at[part, 0]).wait_recv()
    @pl.when(sec == 0)
    def _():
        for part in range(2):
            for mask in range(1, n_rep):
                z_copy(part, mask).wait_send()

    for part in range(2):
        for step in range(len(bits)):
            for mask in kept(part, step + 1):
                sent = rs_send_copy(part, step, mask ^ orders[part][step], local.at[part, 0])
                if step == 0 and mask == ordered(part, 1)[-1]:
                    @pl.when(lent == 1)
                    def _():
                        direct(part).wait_send()
                        via_out(part).wait_send()

                    @pl.when(lent == 0)
                    def _():
                        sent.wait_send()
                else:
                    sent.wait_send()

    @pl.when(sec == 1)
    def _():
        for index in others:
            for part in range(2):
                via_hop(index, part).wait_send()

    for part in range(2):
        base_store(part).wait()

    @pl.loop(0, n_chunks)
    def _(c):
        for i in range(2):
            act_store(c, i).wait()

    @pl.when(sec < last)
    def _():
        @pl.loop(0, n_chunks)
        def _(c):
            for j in range(n_rep):
                f_copy(c, j).wait_send()

    @pl.when(sec > 0)
    def _():
        @pl.loop(0, n_chunks)
        def _(c):
            for j in range(n_rep):
                b_copy(c, j).wait_send()


def finish(rate, u_ref, q_ref, base_ref, far_ref, next_hbm, grad_hbm,
           next_ref, grad_ref, next_sem, grad_sem):
    count, tile = next_ref.shape[:2]

    def next_store(t):
        return pltpu.make_async_copy(
            next_ref.at[t], next_hbm.at[pl.ds(t * tile, tile), :], next_sem.at[t])

    def grad_store(t):
        return pltpu.make_async_copy(
            grad_ref.at[t], grad_hbm.at[pl.ds(t * tile, tile), :], grad_sem.at[t])

    for t in range(count):
        rows = pl.ds(t * tile, tile)
        next_ref[t] = base_ref[rows, :] - rate * far_ref[rows, :].astype(jnp.float32)
        next_store(t).start()
        grad_ref[t] = lax.dot_general(
            u_ref[:, rows], q_ref[...], (((0,), (0,)), ((), ())),
            preferred_element_type=jnp.float32).astype(jnp.bfloat16)
        grad_store(t).start()
    for t in range(count):
        grad_store(t).wait()
        next_store(t).wait()


def body(inputs, cotangent, w_prev, w_now, grads_prev):
    sections = lax.axis_size("section")
    n_rep = lax.axis_size("dp")
    micro, tok_mb, width = inputs.shape
    rows = micro * tok_mb
    cols = width // n_rep
    half = width // 2
    chunk = tok_mb // SPLIT
    n_chunks = rows // chunk
    any_spec = pl.BlockSpec(memory_space=pl.ANY)
    bf16, f32 = jnp.bfloat16, jnp.float32
    dma = pltpu.SemaphoreType.DMA
    rate = learn_rate / n_rep
    upper, small, base, far = pl.pallas_call(
        functools.partial(relay, n_rep, sections, chunk, rate),
        out_shape=(
            jax.ShapeDtypeStruct((rows, width), bf16),
            jax.ShapeDtypeStruct((rows, width), bf16),
            jax.ShapeDtypeStruct((width, cols), f32),
            jax.ShapeDtypeStruct((width, cols), bf16),
        ),
        in_specs=[any_spec] * 5,
        out_specs=(any_spec,) * 4,
        scratch_shapes=[
            pltpu.VMEM((rows, width), bf16),
            pltpu.VMEM((rows, width), bf16),
            pltpu.VMEM((width, cols), f32),
            pltpu.VMEM((n_rep, width, cols), bf16),
            pltpu.VMEM((n_rep, max(cols, rows), width), bf16),
            pltpu.VMEM((n_rep, rows, cols), bf16),
            pltpu.VMEM((n_rep, rows, cols), bf16),
            pltpu.VMEM((n_rep, rows, cols), bf16),
            pltpu.VMEM((n_rep, rows, cols), bf16),
            pltpu.VMEM((n_rep, rows, cols), f32),
            pltpu.VMEM((rows, 1), f32),
            pltpu.VMEM((n_rep, chunk, cols), f32),
            pltpu.VMEM((2, n_rep // 2, half, cols), bf16),
            pltpu.VMEM((2, max(1, n_rep - 2), half, cols), bf16),
            dma((2,)), dma((n_rep,)), dma((n_rep,)), dma((2, n_rep // 2)),
            dma((2, n_rep)), dma((2, n_rep)),
            dma((2, n_rep)), dma((2, n_rep)),
            dma((n_chunks, n_rep)), dma((n_chunks, n_rep)),
            dma((n_chunks, n_rep)), dma((n_chunks, n_rep)),
            dma((2, n_rep)), dma((2, n_rep)),
            dma((2,)), dma((2,)), dma((2, n_chunks)),
            pltpu.VMEM((sections // 2 - 1, 2, half * SHARE // 32, cols), bf16),
            dma((2,)), dma((sections // 2 - 1, 2)), dma((sections // 2 - 1, 2)), dma((2,)),
            pltpu.SemaphoreType.REGULAR, pltpu.SemaphoreType.REGULAR,
        ],
        compiler_params=pltpu.CompilerParams(
            collective_id=0, has_side_effects=True, vmem_limit_bytes=40 * 1024 * 1024
        ),
        name="relay",
    )(*(pltpu.with_memory_space_constraint(array, pltpu.HBM) for array in (
        inputs.reshape(rows, width), cotangent.reshape(rows, width), w_prev[0], grads_prev[0, 0], w_now[0])))
    count = 8
    tile = width // count
    w_next, grads_next = pl.pallas_call(
        functools.partial(finish, rate),
        out_shape=(
            jax.ShapeDtypeStruct((width, cols), f32),
            jax.ShapeDtypeStruct((width, width), bf16),
        ),
        in_specs=[pl.BlockSpec(memory_space=pltpu.VMEM)] * 4,
        out_specs=(any_spec,) * 2,
        scratch_shapes=[
            pltpu.VMEM((count, tile, cols), f32),
            pltpu.VMEM((count, tile, width), bf16),
            dma((count,)), dma((count,)),
        ],
        compiler_params=pltpu.CompilerParams(vmem_limit_bytes=24 * 1024 * 1024),
        name="finish",
    )(upper, small, base, far)
    return (w_next[None], grads_next[None, None])


def solution(mesh):
    return jax.shard_map(
        body,
        mesh=mesh,
        in_specs=(
            P(None, "dp", None),
            P(None, "dp", None),
            P("section", None, "dp"),
            P("section", None, "dp"),
            P("dp", "section", None, None),
        ),
        out_specs=(P("section", None, "dp"), P("dp", "section", None, None)),
        check_vma=False,
    )
```

```python
import functools

import jax
import jax.numpy as jnp
from jax import lax
from jax.experimental import pallas as pl
from jax.experimental.pallas import tpu as pltpu
from jax.sharding import PartitionSpec as P

norm_eps = 1e-06
learn_rate = 1.0
MESH = pl.DeviceIdType.MESH
SPLIT = 2
SHARE = 5


def flipped(me, mask):
    out, bit, left = me, 1, mask
    while left:
        if left & 1:
            out = out + bit * (1 - 2 * ((me // bit) % 2))
        left >>= 1
        bit <<= 1
    return out


def spans(order):
    masks = [0]
    for bit in order:
        masks = masks + [mask ^ bit for mask in masks]
    return masks


def relay(n_rep, sections, chunk, rate, x_hbm, cot_hbm, w_hbm, g_hbm, now_hbm,
          u_hbm, q_hbm, base_hbm, far_hbm,
          u_ref, q_ref, wf, weight, turned, xin, dyin, ybuf, dxbuf, zbuf, rbuf, dubuf, local, landed,
          load_sem, x_sem, cot_sem, local_sem,
          ag_send, ag_recv, rs_send, rs_recv, f_send, f_recv, b_send, b_recv,
          z_send, z_recv, now_sem, base_sem, act_sem,
          stage, via_send, stage_recv, hop_send, via_recv, gate, back):
    me = lax.axis_index("dp")
    sec = lax.axis_index("section")
    last = sections - 1
    rows, width = x_hbm.shape
    cols = width // n_rep
    half = width // 2
    n_chunks = rows // chunk
    inv = width ** (-0.5)
    fill = half // 4
    share = half * SHARE // 32
    others = range(sections // 2 - 1)
    lent = (sec % 2) * ((sec + sections - 3) // sections)
    bits = [1 << i for i in range(n_rep.bit_length() - 1)]
    orders = (bits, bits[::-1])

    for part in range(2):
        sl = pl.ds(part * half, half)
        copy = pltpu.make_async_copy(w_hbm.at[sl, :], wf.at[sl, :], load_sem.at[part])
        copy.start()

    def x_load(j):
        return pltpu.make_async_copy(
            x_hbm.at[:, pl.ds(j * cols, cols)], xin.at[j], x_sem.at[j])

    def cot_load(j):
        return pltpu.make_async_copy(
            cot_hbm.at[:, pl.ds(j * cols, cols)], dyin.at[j], cot_sem.at[j])

    @pl.when(sec == 0)
    def _():
        for j in range(n_rep):
            x_load(j).start()

    @pl.when(sec == last)
    def _():
        for j in range(n_rep):
            cot_load(j).start()

    def g_block(part, mask):
        at = pl.multiple_of(flipped(me, mask) * cols, cols)
        return g_hbm.at[pl.ds(part * half, half), pl.ds(at, cols)]

    barrier = pltpu.get_barrier_semaphore()
    for mask in range(1, n_rep):
        pl.semaphore_signal(barrier, inc=1, device_id={"dp": flipped(me, mask)}, device_id_type=MESH)

    @pl.when(sec > 0)
    def _():
        pl.semaphore_signal(barrier, inc=1, device_id={"section": sec - 1}, device_id_type=MESH)

    @pl.when(sec < last)
    def _():
        pl.semaphore_signal(barrier, inc=1, device_id={"section": sec + 1}, device_id_type=MESH)

    firsts = sorted({orders[0][0], orders[1][0]})

    @pl.when(sec == 1)
    def _():
        for index in others:
            for bit in firsts:
                pl.semaphore_signal(
                    barrier, inc=1, device_id={"dp": flipped(me, bit), "section": 2 * index + 3},
                    device_id_type=MESH)

    @pl.when(lent == 1)
    def _():
        pl.semaphore_signal(barrier, inc=1, device_id={"section": 1}, device_id_type=MESH)

    neighbours = (sec + last) // sections + (2 * last - sec) // sections
    helpers = lent * len(firsts) + (sec % 2) * (1 - lent) * len(others)
    pl.semaphore_wait(barrier, n_rep - 1 + neighbours + helpers)

    def piece_of(tokens, part, mask):
        if tokens:
            return turned.at[flipped(me, mask), pl.ds(part * (rows // 2), rows // 2), :]
        return weight.at[flipped(me, mask), pl.ds(part * half, half), :]

    def ag_copy(tokens, part, mask, bit):
        ref = piece_of(tokens, part, mask)
        return pltpu.make_async_remote_copy(
            src_ref=ref, dst_ref=ref,
            send_sem=ag_send.at[part, mask ^ bit], recv_sem=ag_recv.at[part, mask ^ bit],
            device_id={"dp": flipped(me, bit)}, device_id_type=MESH)

    def ag_arrival(tokens, part, mask):
        ref = piece_of(tokens, part, mask)
        return pltpu.make_async_remote_copy(
            src_ref=ref, dst_ref=ref,
            send_sem=ag_send.at[part, mask], recv_sem=ag_recv.at[part, mask],
            device_id={"dp": flipped(me, mask)}, device_id_type=MESH)

    def gather(tokens, prepare):
        for part in range(2):
            prepare(part)
            ag_copy(tokens, part, 0, orders[part][0]).start()
        for step in range(1, len(bits)):
            for part in range(2):
                ag_copy(tokens, part, 0, orders[part][step]).start()
        arrived = set()
        for step in range(1, len(bits)):
            for index in range(1, 1 << step):
                for part in range(2):
                    this = spans(orders[part][:step])[index]
                    if (part, this) not in arrived:
                        ag_arrival(tokens, part, this).wait_recv()
                        arrived.add((part, this))
                    ag_copy(tokens, part, this, orders[part][step]).start()
        return arrived

    def gather_sent(tokens, masks):
        for part in range(2):
            for mask in masks:
                ag_copy(tokens, part, 0, mask).wait_send()

    everyone = range(1, n_rep)
    relayed = [mask for mask in everyone if mask not in bits]

    def cast(part):
        pltpu.make_async_copy(
            w_hbm.at[pl.ds(part * half, half), :], wf.at[pl.ds(part * half, half), :],
            load_sem.at[part]).wait()
        piece = half // 4
        for i in range(4):
            sl = pl.ds(part * half + i * piece, piece)
            weight[me, sl, :] = wf[sl, :].astype(jnp.bfloat16)

    def normalise(sl):
        square = jnp.zeros((chunk, 1), jnp.float32)
        for j in range(n_rep):
            x = xin[j, sl, :].astype(jnp.float32)
            square += jnp.sum(x * x, axis=-1, keepdims=True)
        scale = lax.rsqrt(square * (1.0 / width) + norm_eps)
        rbuf[sl, :] = scale
        for j in range(n_rep):
            x = xin[j, sl, :].astype(jnp.float32)
            u_ref[sl, pl.ds(j * cols, cols)] = (x * scale).astype(jnp.bfloat16)

    def z_copy(part, mask):
        sl = pl.ds(part * (rows // 2), rows // 2)
        return pltpu.make_async_remote_copy(
            src_ref=dxbuf.at[mask, sl, :], dst_ref=dyin.at[me, sl, :],
            send_sem=z_send.at[part, mask], recv_sem=z_recv.at[part, mask],
            device_id={"dp": flipped(me, mask)}, device_id_type=MESH)

    def z_arrival(part, mask):
        sl = pl.ds(part * (rows // 2), rows // 2)
        return pltpu.make_async_remote_copy(
            src_ref=dxbuf.at[mask, sl, :], dst_ref=dyin.at[flipped(me, mask), sl, :],
            send_sem=z_send.at[part, mask], recv_sem=z_recv.at[part, mask],
            device_id={"dp": flipped(me, mask)}, device_id_type=MESH)

    odd = lax.rem(sec, 2) == 1

    def rs_send_copy(part, step, mask, source):
        bit = orders[part][step]
        slot = mask ^ bit
        if step == len(bits) - 1:
            target = far_hbm.at[pl.ds(part * half, half), :]
        else:
            target = landed.at[part, slot_of(part, step, slot)]
        return pltpu.make_async_remote_copy(
            src_ref=source, dst_ref=target,
            send_sem=rs_send.at[part, slot_of(part, step, slot)],
            recv_sem=rs_recv.at[part, slot_of(part, step, slot)],
            device_id={"dp": flipped(me, bit)}, device_id_type=MESH)

    def kept(part, step):
        return sorted(spans(orders[part][step:]))

    def ordered(part, step):
        return sorted(kept(part, step), key=lambda mask: (not mask & orders[part][step], mask))

    def slot_of(part, step, mask):
        base = sum(len(kept(part, s + 1)) for s in range(step))
        return base + kept(part, step + 1).index(mask)

    def local_copy(part, mask):
        at = kept(part, 1).index(mask)
        return pltpu.make_async_copy(
            g_block(part, mask), local.at[part, at], local_sem.at[part, at])

    def rs_rows(part, mask, low, high):
        span = pl.ds(low, high - low)
        slot = slot_of(part, 0, mask ^ orders[part][0])
        pltpu.make_async_remote_copy(
            src_ref=g_block(part, mask).at[span, :], dst_ref=landed.at[part, slot, span, :],
            send_sem=rs_send.at[part, slot], recv_sem=rs_recv.at[part, slot],
            device_id={"dp": flipped(me, orders[part][0])}, device_id_type=MESH).start()

    def rs_early():
        for part in range(2):
            rs_rows(part, ordered(part, 1)[-1] ^ orders[part][0], 0, fill)

    def via_out(part):
        mask = ordered(part, 1)[-1] ^ orders[part][0]
        return pltpu.make_async_remote_copy(
            src_ref=g_block(part, mask).at[pl.ds(half - share, share), :],
            dst_ref=stage.at[jnp.maximum(sec // 2 - 1, 0), part],
            send_sem=via_send.at[part], recv_sem=stage_recv.at[jnp.maximum(sec // 2 - 1, 0), part],
            device_id={"dp": flipped(me, orders[part][0]), "section": 1}, device_id_type=MESH)

    def via_hop(index, part):
        slot = slot_of(part, 0, ordered(part, 1)[-1])
        return pltpu.make_async_remote_copy(
            src_ref=stage.at[index, part],
            dst_ref=landed.at[part, slot, pl.ds(half - share, share), :],
            send_sem=hop_send.at[index, part], recv_sem=via_recv.at[part],
            device_id={"section": 2 * index + 3}, device_id_type=MESH)

    def via_stage(index, part):
        return pltpu.make_async_remote_copy(
            src_ref=stage.at[index, part], dst_ref=stage.at[index, part],
            send_sem=hop_send.at[index, part], recv_sem=stage_recv.at[index, part],
            device_id={"section": 2 * index + 3}, device_id_type=MESH)

    def direct(part):
        slot = slot_of(part, 0, ordered(part, 1)[-1])
        span = pl.ds(0, half - share)
        return pltpu.make_async_remote_copy(
            src_ref=landed.at[part, slot, span, :], dst_ref=landed.at[part, slot, span, :],
            send_sem=rs_send.at[part, slot], recv_sem=rs_recv.at[part, slot],
            device_id={"dp": flipped(me, orders[part][0])}, device_id_type=MESH)

    def rs_start(done, high):
        for mask_at in range(n_rep // 2):
            for part in range(2):
                mask = ordered(part, 1)[mask_at] ^ orders[part][0]
                stays = mask_at == n_rep // 2 - 1
                rs_rows(part, mask, done if stays else 0, high if stays else half)
        for part in range(2):
            for mask in ordered(part, 1):
                local_copy(part, mask).start()

    @pl.when(odd & (sec > 1))
    def _():
        rs_early()

    def turn():
        @pl.loop(0, n_rep)
        def _(j):
            for k in range(n_rep):
                span = pl.ds(k * cols, cols)
                turned[j, pl.ds(0, cols), span] = weight[j, span, :].T

    @pl.when(sec == 0)
    def _():
        for j in range(n_rep):
            x_load(j).wait()

        def prepare(part):
            @pl.loop(part * (n_chunks // 2), (part + 1) * (n_chunks // 2))
            def _(c):
                sl = pl.ds(pl.multiple_of(c * chunk, chunk), chunk)
                normalise(sl)
                turned[me, sl, :] = u_ref[sl, :]

        arrived = gather(True, prepare)
        for part in range(2):
            cast(part)
        for mask in range(n_rep):
            for part in range(2):
                if mask and (part, mask) not in arrived:
                    ag_arrival(True, part, mask).wait_recv()
                sl = pl.ds(part * (rows // 2), rows // 2)
                z = jnp.dot(turned[flipped(me, mask), sl, :], weight[me],
                            preferred_element_type=jnp.float32) * inv
                if mask:
                    dxbuf[mask, sl, :] = z.astype(jnp.bfloat16)
                    z_copy(part, mask).start()
                else:
                    zbuf[me, sl, :] = z
        gather_sent(True, everyone)

    @pl.when((sec > 0) & jnp.logical_not(odd))
    def _():
        arrived = gather(False, cast)
        gather_sent(False, bits)
        pl.semaphore_signal(
            gate, inc=1, device_id={"section": jnp.minimum(sec + 1, last)}, device_id_type=MESH)
        gather_sent(False, relayed)
        for part in range(2):
            for mask in range(1, n_rep):
                if (part, mask) not in arrived:
                    ag_arrival(False, part, mask).wait_recv()
        turn()

    early = sections // 2

    @pl.when(odd)
    def _():
        @pl.when(sec > 1)
        def _():
            pl.semaphore_wait(gate, 1)

        arrived = gather(False, cast)

        @pl.when(sec == 1)
        def _():
            rs_early()

        @pl.when(sec >= 2)
        def _():
            for part in range(2):
                via_out(part).start()
            rs_start(fill, half - share)

        gather_sent(False, everyone)
        pl.semaphore_signal(
            back, inc=1, device_id={"section": jnp.maximum(sec - 1, 0)}, device_id_type=MESH)

        @pl.when(sec < 2)
        def _():
            rs_start(fill, half)

        for part in range(2):
            for mask in range(1, n_rep):
                if (part, mask) not in arrived:
                    ag_arrival(False, part, mask).wait_recv()

    @pl.when(odd & (sec >= early))
    def _():
        turn()

    @pl.when(jnp.logical_not(odd) & (sec >= early))
    def _():
        pl.semaphore_wait(back, 1)
        rs_start(0, half)

    def now_load(part):
        sl = pl.ds(part * half, half)
        return pltpu.make_async_copy(now_hbm.at[sl, :], wf.at[sl, :], now_sem.at[part])

    def base_store(part):
        sl = pl.ds(part * half, half)
        return pltpu.make_async_copy(wf.at[sl, :], base_hbm.at[sl, :], base_sem.at[part])

    def act_store(c, i):
        sl = pl.ds(pl.multiple_of(c * chunk, chunk), chunk)
        source, target = ((u_ref, u_hbm), (q_ref, q_hbm))[i]
        return pltpu.make_async_copy(source.at[sl, :], target.at[sl, :], act_sem.at[i, c])

    for part in range(2):
        now_load(part).start()

    def f_copy(c, j):
        sl = pl.ds(pl.multiple_of(c * chunk, chunk), chunk)
        return pltpu.make_async_remote_copy(
            src_ref=ybuf.at[j, sl, :], dst_ref=xin.at[j, sl, :],
            send_sem=f_send.at[c, j], recv_sem=f_recv.at[c, j],
            device_id={"section": jnp.minimum(sec + 1, last)}, device_id_type=MESH)

    def b_copy(c, j):
        sl = pl.ds(pl.multiple_of(c * chunk, chunk), chunk)
        return pltpu.make_async_remote_copy(
            src_ref=dxbuf.at[j, sl, :], dst_ref=dyin.at[j, sl, :],
            send_sem=b_send.at[c, j], recv_sem=b_recv.at[c, j],
            device_id={"section": jnp.maximum(sec - 1, 0)}, device_id_type=MESH)

    @pl.when(sec == 0)
    def _():
        for part in range(2):
            for mask in range(1, n_rep):
                z_arrival(part, mask).wait_recv()
                sl = pl.ds(part * (rows // 2), rows // 2)
                zbuf[flipped(me, mask), sl, :] = dyin[flipped(me, mask), sl, :].astype(jnp.float32)

    @pl.when(sec == last)
    def _():
        for j in range(n_rep):
            cot_load(j).wait()

    def section_input(c):
        for j in range(n_rep):
            f_copy(c, j).wait_recv()
        normalise(pl.ds(pl.multiple_of(c * chunk, chunk), chunk))

    def project(c, j):
        sl = pl.ds(pl.multiple_of(c * chunk, chunk), chunk)
        zbuf[j, sl, :] = jnp.dot(
            u_ref[sl, :], weight[j], preferred_element_type=jnp.float32) * inv

    def emit(c, j):
        sl = pl.ds(pl.multiple_of(c * chunk, chunk), chunk)
        zz = zbuf[j, sl, :]
        y = xin[j, sl, :].astype(jnp.float32) + zz * jax.nn.sigmoid(zz)
        ybuf[j, sl, :] = y.astype(jnp.bfloat16)
        f_copy(c, j).start()

    def small_grad(c, j):
        sl = pl.ds(pl.multiple_of(c * chunk, chunk), chunk)
        z = zbuf[j, sl, :]
        sig = jax.nn.sigmoid(z)
        dz = dyin[j, sl, :].astype(jnp.float32) * sig * (1.0 + z * (1.0 - sig))
        q_ref[sl, pl.ds(j * cols, cols)] = (dz * inv).astype(jnp.bfloat16)

    def back_project(c, j):
        sl = pl.ds(pl.multiple_of(c * chunk, chunk), chunk)
        q = q_ref[sl, pl.ds(j * cols, cols)]
        for k in range(n_rep):
            du = jnp.dot(q, turned[j, pl.ds(0, cols), pl.ds(k * cols, cols)], preferred_element_type=jnp.float32)
            dubuf[k] = du if j == 0 else dubuf[k] + du

    def emit_back(c):
        sl = pl.ds(pl.multiple_of(c * chunk, chunk), chunk)
        scale = rbuf[sl, :]
        dot_sum = jnp.zeros((chunk, 1), jnp.float32)
        for k in range(n_rep):
            normed = xin[k, sl, :].astype(jnp.float32) * scale
            dot_sum += jnp.sum(dubuf[k] * normed, axis=-1, keepdims=True)
        mean = dot_sum * (1.0 / width)
        for k in range(n_rep):
            normed = xin[k, sl, :].astype(jnp.float32) * scale
            dx = dyin[k, sl, :].astype(jnp.float32) + scale * (dubuf[k] - normed * mean)
            dxbuf[k, sl, :] = dx.astype(jnp.bfloat16)
            b_copy(c, k).start()
        for i in range(2):
            act_store(c, i).start()

    middle = (sec > 0) & (sec < last)

    @pl.when(sec == 0)
    def _():
        @pl.loop(0, n_chunks)
        def _(c):
            for j in range(n_rep):
                emit(c, j)

    @pl.when(middle)
    def _():
        @pl.loop(0, n_chunks)
        def _(c):
            section_input(c)
            for j in range(n_rep):
                project(c, j)
                emit(c, j)

    def rs_add(step, part, mask):
        arrival = rs_send_copy(part, step - 1, mask ^ orders[part][step - 1], landed.at[part, 0])
        if step == 1 and mask == ordered(part, 1)[-1]:
            @pl.when(lent == 1)
            def _():
                direct(part).wait_recv()
                via_hop(0, part).wait_recv()

            @pl.when(lent == 0)
            def _():
                arrival.wait_recv()
        else:
            arrival.wait_recv()
        at = kept(part, 1).index(mask)
        if step == 1:
            local_copy(part, mask).wait()
        if step == 1 and not mask:
            now_load(part).wait()
        pieces = 4
        piece = half // pieces
        for i in range(pieces):
            ps = pl.ds(i * piece, piece)
            total = landed[part, slot_of(part, step - 1, mask), ps, :].astype(jnp.float32)
            if step == 1:
                total = local[part, at, ps, :].astype(jnp.float32) + total
            elif mask:
                total = local[part, at, ps, :].astype(jnp.float32) + total
            if mask:
                local[part, at, ps, :] = total.astype(jnp.bfloat16)
            else:
                held = pl.ds(part * half + i * piece, piece)
                wf[held, :] = wf[held, :] - rate * total
        if not mask and step == len(bits) - 1:
            base_store(part).start()
        if mask & orders[part][step]:
            rs_send_copy(part, step, mask, local.at[part, at]).start()

    def rs_middle(first):
        for step in range(1, len(bits)):
            for index in range(len(kept(0, step))):
                for part in range(2):
                    mask = ordered(part, step)[index]
                    if first == (step == 1 and mask & orders[part][1] > 0):
                        rs_add(step, part, mask)

    @pl.when(odd & (sec < early))
    def _():
        turn()

    @pl.when(jnp.logical_not(odd) & (sec < early))
    def _():
        pl.semaphore_wait(back, 1)
        rs_start(0, half)

    @pl.when(sec < early)
    def _():
        rs_middle(True)

    @pl.when(sec == 1)
    def _():
        for index in others:
            for part in range(2):
                via_stage(index, part).wait_recv()
                via_hop(index, part).start()

    @pl.when(sec == 0)
    def _():
        @pl.loop(0, n_chunks)
        def _(c):
            for j in range(n_rep):
                b_copy(c, j).wait_recv()
                small_grad(c, j)
            for i in range(2):
                act_store(c, i).start()

    @pl.when(middle)
    def _():
        @pl.loop(0, n_chunks)
        def _(c):
            for j in range(n_rep):
                b_copy(c, j).wait_recv()
                small_grad(c, j)
                back_project(c, j)
            emit_back(c)

            @pl.when((c == 0) & (sec >= early) & (sec < sections - 2))
            def _():
                rs_middle(True)

    @pl.when(sec == last)
    def _():
        @pl.loop(0, n_chunks)
        def _(c):
            section_input(c)
            for j in range(n_rep):
                project(c, j)
            for j in range(n_rep):
                small_grad(c, j)
                back_project(c, j)
            emit_back(c)

    @pl.when(sec >= sections - 2)
    def _():
        rs_middle(True)

    rs_middle(False)

    final = len(bits) - 1
    for part in range(2):
        rs_send_copy(part, final, orders[part][final], local.at[part, 0]).wait_recv()
    @pl.when(sec == 0)
    def _():
        for part in range(2):
            for mask in range(1, n_rep):
                z_copy(part, mask).wait_send()

    for part in range(2):
        for step in range(len(bits)):
            for mask in kept(part, step + 1):
                sent = rs_send_copy(part, step, mask ^ orders[part][step], local.at[part, 0])
                if step == 0 and mask == ordered(part, 1)[-1]:
                    @pl.when(lent == 1)
                    def _():
                        direct(part).wait_send()
                        via_out(part).wait_send()

                    @pl.when(lent == 0)
                    def _():
                        sent.wait_send()
                else:
                    sent.wait_send()

    @pl.when(sec == 1)
    def _():
        for index in others:
            for part in range(2):
                via_hop(index, part).wait_send()

    for part in range(2):
        base_store(part).wait()

    @pl.loop(0, n_chunks)
    def _(c):
        for i in range(2):
            act_store(c, i).wait()

    @pl.when(sec < last)
    def _():
        @pl.loop(0, n_chunks)
        def _(c):
            for j in range(n_rep):
                f_copy(c, j).wait_send()

    @pl.when(sec > 0)
    def _():
        @pl.loop(0, n_chunks)
        def _(c):
            for j in range(n_rep):
                b_copy(c, j).wait_send()


def finish(rate, u_ref, q_ref, base_ref, far_ref, next_hbm, grad_hbm,
           next_ref, grad_ref, next_sem, grad_sem):
    count, tile = next_ref.shape[:2]

    def next_store(t):
        return pltpu.make_async_copy(
            next_ref.at[t], next_hbm.at[pl.ds(t * tile, tile), :], next_sem.at[t])

    def grad_store(t):
        return pltpu.make_async_copy(
            grad_ref.at[t], grad_hbm.at[pl.ds(t * tile, tile), :], grad_sem.at[t])

    for t in range(count):
        rows = pl.ds(t * tile, tile)
        next_ref[t] = base_ref[rows, :] - rate * far_ref[rows, :].astype(jnp.float32)
        next_store(t).start()
        grad_ref[t] = lax.dot_general(
            u_ref[:, rows], q_ref[...], (((0,), (0,)), ((), ())),
            preferred_element_type=jnp.float32).astype(jnp.bfloat16)
        grad_store(t).start()
    for t in range(count):
        grad_store(t).wait()
        next_store(t).wait()


def body(inputs, cotangent, w_prev, w_now, grads_prev):
    sections = lax.axis_size("section")
    n_rep = lax.axis_size("dp")
    micro, tok_mb, width = inputs.shape
    rows = micro * tok_mb
    cols = width // n_rep
    half = width // 2
    chunk = tok_mb // SPLIT
    n_chunks = rows // chunk
    any_spec = pl.BlockSpec(memory_space=pl.ANY)
    bf16, f32 = jnp.bfloat16, jnp.float32
    dma = pltpu.SemaphoreType.DMA
    rate = learn_rate / n_rep
    upper, small, base, far = pl.pallas_call(
        functools.partial(relay, n_rep, sections, chunk, rate),
        out_shape=(
            jax.ShapeDtypeStruct((rows, width), bf16),
            jax.ShapeDtypeStruct((rows, width), bf16),
            jax.ShapeDtypeStruct((width, cols), f32),
            jax.ShapeDtypeStruct((width, cols), bf16),
        ),
        in_specs=[any_spec] * 5,
        out_specs=(any_spec,) * 4,
        scratch_shapes=[
            pltpu.VMEM((rows, width), bf16),
            pltpu.VMEM((rows, width), bf16),
            pltpu.VMEM((width, cols), f32),
            pltpu.VMEM((n_rep, width, cols), bf16),
            pltpu.VMEM((n_rep, max(cols, rows), width), bf16),
            pltpu.VMEM((n_rep, rows, cols), bf16),
            pltpu.VMEM((n_rep, rows, cols), bf16),
            pltpu.VMEM((n_rep, rows, cols), bf16),
            pltpu.VMEM((n_rep, rows, cols), bf16),
            pltpu.VMEM((n_rep, rows, cols), f32),
            pltpu.VMEM((rows, 1), f32),
            pltpu.VMEM((n_rep, chunk, cols), f32),
            pltpu.VMEM((2, n_rep // 2, half, cols), bf16),
            pltpu.VMEM((2, max(1, n_rep - 2), half, cols), bf16),
            dma((2,)), dma((n_rep,)), dma((n_rep,)), dma((2, n_rep // 2)),
            dma((2, n_rep)), dma((2, n_rep)),
            dma((2, n_rep)), dma((2, n_rep)),
            dma((n_chunks, n_rep)), dma((n_chunks, n_rep)),
            dma((n_chunks, n_rep)), dma((n_chunks, n_rep)),
            dma((2, n_rep)), dma((2, n_rep)),
            dma((2,)), dma((2,)), dma((2, n_chunks)),
            pltpu.VMEM((sections // 2 - 1, 2, half * SHARE // 32, cols), bf16),
            dma((2,)), dma((sections // 2 - 1, 2)), dma((sections // 2 - 1, 2)), dma((2,)),
            pltpu.SemaphoreType.REGULAR, pltpu.SemaphoreType.REGULAR,
        ],
        compiler_params=pltpu.CompilerParams(
            collective_id=0, has_side_effects=True, vmem_limit_bytes=40 * 1024 * 1024
        ),
        name="relay",
    )(*(pltpu.with_memory_space_constraint(array, pltpu.HBM) for array in (
        inputs.reshape(rows, width), cotangent.reshape(rows, width), w_prev[0], grads_prev[0, 0], w_now[0])))
    count = 8
    tile = width // count
    w_next, grads_next = pl.pallas_call(
        functools.partial(finish, rate),
        out_shape=(
            jax.ShapeDtypeStruct((width, cols), f32),
            jax.ShapeDtypeStruct((width, width), bf16),
        ),
        in_specs=[pl.BlockSpec(memory_space=pltpu.VMEM)] * 4,
        out_specs=(any_spec,) * 2,
        scratch_shapes=[
            pltpu.VMEM((count, tile, cols), f32),
            pltpu.VMEM((count, tile, width), bf16),
            dma((count,)), dma((count,)),
        ],
        compiler_params=pltpu.CompilerParams(vmem_limit_bytes=24 * 1024 * 1024),
        name="finish",
    )(upper, small, base, far)
    return (w_next[None], grads_next[None, None])


def solution(mesh):
    return jax.shard_map(
        body,
        mesh=mesh,
        in_specs=(
            P(None, "dp", None),
            P(None, "dp", None),
            P("section", None, "dp"),
            P("section", None, "dp"),
            P("dp", "section", None, None),
        ),
        out_specs=(P("section", None, "dp"), P("dp", "section", None, None)),
        check_vma=False,
    )
```
